512 devices in a mesh: ty: 16 (over x_hi, y), tx: 32 (over x_lo, z, core).
Axes of the slice: x: 4 (x_hi: 2, x_lo: 2; x = x_hi * 2 + x_lo), y: 8, z: 8, core: 2. Of those that a mesh axis runs over, the one named last changes fastest.
Arguments:
- ensemble: bfloat16 [32, 8, 128, 4096], P('tx', None, 'ty'), may hold values from -6 to 6
- diffusivity: float32 [128, 4096], P('ty', 'tx'), may hold values from 0.1 to 0.245
- vertical: float32 [8, 8], replicated, as said below
- weights: float32 [32], replicated, may hold values from 0.015625 to 0.0625
- obs_value: float32 [512, 32, 8], P(('ty', 'tx')), may hold values from -6 to 6
- obs_cell: int32 [512, 32, 8], P(('ty', 'tx')), may hold values from 0 to 8191
- obs_count: int32 [512, 32], P(('ty', 'tx')), may hold values from 0 to 8, as said below
Outputs:
- increment: float32 [8, 128, 4096], P(None, 'ty', 'tx')
- projected: float32 [512, 32, 8], P(('ty', 'tx'))
The draws below stay inside these ranges and needn't reach their ends.
Inputs may be any that keep to these rules, and one draw needn't show every extreme that they name: `obs_count`: in every tile row one destination column, drawn from the seed, receives 8 live slots from every source of that row; other loads are uneven across destination columns. `vertical`: Banded: entries more than two levels off the diagonal are zero.
All inputs are finite; a program needn't handle non-finite values.
Results may differ from the reference program's by a relative error of at most 0.0003.
Values may be sent and summed in bfloat16 or wider, within the bound.
A program may use at most 64 MiB of HBM per device.

```python
import math
import jax
import jax.numpy as jnp
from jax import lax

LEVELS = 8
TILE_ROWS = 8
TILE_COLS = 128
STEPS = 4
SLOTS = 8
MEMBERS = 32
ROWS = 128
COLS = 4096
TILES_X = 32
TILES_Y = 16
SOURCES = 512


def draw_vertical(key, part):
    first, second = jax.random.split(key)
    diag_part = jax.random.uniform(first, (LEVELS,), jnp.float32, 1.0, 1.5)
    off_part = jax.random.uniform(second, (LEVELS, LEVELS), jnp.float32, -0.25, 0.25)
    rows_idx = jnp.arange(LEVELS)[:, None]
    cols_idx = jnp.arange(LEVELS)[None, :]
    gap_size = jnp.abs(rows_idx - cols_idx)
    banded = jnp.where((gap_size > 0) & (gap_size <= 2), off_part, jnp.float32(0.0))
    return banded + jnp.diag(diag_part)


def draw_obs_count(key, part):
    first, second, third = jax.random.split(key, 3)
    factor = jax.random.randint(first, (TILES_X,), 1, 5)
    base_load = jax.random.randint(second, (SOURCES, TILES_X), 0, SLOTS // 2 + 1)
    loads = jnp.minimum(base_load * factor[None, :], SLOTS)
    full_col = jax.random.randint(third, (TILES_Y,), 0, TILES_X)
    src_row = jnp.arange(SOURCES) // TILES_X
    hit_col = jnp.arange(TILES_X)[None, :] == full_col[src_row][:, None]
    return jnp.where(hit_col, SLOTS, loads).astype(jnp.int32)


def with_ends(values, key, smallest, largest):
    longest = values.shape.index(max(values.shape))
    spots = []
    for shift in (0, 1):
        where = [jax.random.randint(jax.random.fold_in(key, axis), (), 0, length) for axis, length in enumerate(values.shape)]
        where[longest] = (where[longest] + shift) % values.shape[longest]
        spots.append(tuple(where))
    return values.at[spots[0]].set(smallest).at[spots[1]].set(largest)


def steps_of(rng, extent, cuts, low, largest):
    loudness, own = 1.0, jax.random.fold_in(rng, 6)
    for dim, blocks in cuts:
        steps = jnp.exp(jax.random.uniform(jax.random.fold_in(own, dim), (blocks,), jnp.float32, low / len(cuts), largest / len(cuts)))
        loudness = loudness * jnp.repeat(steps, extent[dim] // blocks).reshape([-1 if axis == dim else 1 for axis in range(len(extent))])
    return loudness


def bell_draw(key, extent, width, limit, pieces=(), held_as=jnp.bfloat16):
    factor_of = steps_of(key, extent, pieces, -0.22, 0.18) if pieces else 1.0
    drawn = jax.random.normal(key, extent, jnp.float32) * width * factor_of
    return jnp.minimum(jnp.maximum(drawn, -limit), limit).astype(held_as)


def setup_inputs(seed: int = 0) -> dict:
    key_list = jax.random.split(jax.random.key(seed), 8)
    ensemble = bell_draw(key_list[0], (MEMBERS, LEVELS, ROWS, COLS), 1.0, 6.0, ((0, 32), (2, 16)))
    diffusivity = jnp.clip(jnp.exp(math.log(0.245) - 0.896088 * jax.random.uniform(key_list[1], (ROWS, COLS), jnp.float32) ** steps_of(key_list[1], (ROWS, COLS), ((0, 16), (1, 32)), -0.2, 0.2)), 0.1, 0.245)
    vertical = draw_vertical(jax.random.fold_in(key_list[7], 71), 0)
    weights = jnp.clip(jnp.exp(jax.random.uniform(key_list[3], (MEMBERS,), jnp.float32, math.log(0.015625), math.log(0.0625))), 0.015625, 0.0625)
    obs_value = bell_draw(key_list[4], (SOURCES, TILES_X, SLOTS), 1.0, 6.0, ((0, 512),), jnp.float32)
    obs_cell = with_ends(jax.random.randint(key_list[5], (SOURCES, TILES_X, SLOTS), 0, LEVELS * TILE_ROWS * TILE_COLS), jax.random.fold_in(key_list[5], 1), 0, (LEVELS * TILE_ROWS * TILE_COLS) - 1).astype(jnp.int32)
    obs_count = draw_obs_count(jax.random.fold_in(key_list[7], 71), 0)
    return dict(ensemble=ensemble, diffusivity=diffusivity, vertical=vertical, weights=weights, obs_value=obs_value, obs_cell=obs_cell, obs_count=obs_count)


def diffuse(current, diffusivity):
    padded = jnp.pad(current, ((0, 0), (1, 1), (1, 1)))
    beside = padded[:, :-2, 1:-1] + padded[:, 2:, 1:-1] + padded[:, 1:-1, :-2] + padded[:, 1:-1, 2:]
    return current + diffusivity * (beside - 4.0 * current)


def reference(ensemble, diffusivity, vertical, weights, obs_value, obs_cell, obs_count):
    tile_cells = TILE_ROWS * TILE_COLS
    source = jnp.arange(SOURCES, dtype=jnp.int32)
    tile_row = source // TILES_X
    dest_col = jnp.arange(TILES_X, dtype=jnp.int32)
    level_of = obs_cell // tile_cells
    in_tile = obs_cell % tile_cells
    glob_row = tile_row[:, None, None] * TILE_ROWS + in_tile // TILE_COLS
    glob_col = dest_col[None, :, None] * TILE_COLS + in_tile % TILE_COLS
    live_slots = jnp.arange(SLOTS, dtype=jnp.int32)[None, None, :] < obs_count[:, :, None]
    flat_index = ((level_of * ROWS + glob_row) * COLS + glob_col).astype(jnp.int32)
    forcing = jnp.zeros((LEVELS * ROWS * COLS,), jnp.float32)
    forcing = forcing.at[flat_index.ravel()].add(jnp.where(live_slots, obs_value, jnp.float32(0.0)).ravel())
    forcing = forcing.reshape(LEVELS, ROWS, COLS)

    def add_member(accum_sum, inputs):
        member, weight = inputs
        perturb = member.astype(jnp.float32)
        current = perturb * forcing
        for repeat in range(STEPS):
            current = diffuse(current, diffusivity)
        current = jnp.einsum("lm,mrc->lrc", vertical, current, precision=lax.Precision.HIGHEST)
        return accum_sum + weight * perturb * current, None

    result, unused = lax.scan(add_member, jnp.zeros((LEVELS, ROWS, COLS), jnp.float32), (ensemble, weights))
    projected = jnp.where(live_slots, result.ravel()[flat_index], jnp.float32(0.0))
    return result, projected
```

```python
import functools

import jax
import jax.numpy as jnp
from jax import lax
from jax.experimental import pallas as pl
from jax.experimental.pallas import tpu as pltpu
from jax.sharding import PartitionSpec as P

STEPS = 4
HALO = 4
LANES = 128
GROUP = 16
CHUNKS = 2
MESH = pl.DeviceIdType.MESH
DIRS = ((-1, -1), (-1, 0), (-1, 1), (0, -1), (0, 1), (1, -1), (1, 0), (1, 1))
UP, DOWN, LEFT, RIGHT = 1, 6, 3, 4


def split3(x):
    hi = x.astype(jnp.bfloat16)
    rest = x - hi.astype(jnp.float32)
    mid = rest.astype(jnp.bfloat16)
    low = (rest - mid.astype(jnp.float32)).astype(jnp.bfloat16)
    return hi, mid, low


def diffused(own, halo, coef_own, coef_halo, keep_own, keep_halo, first, last):
    for _ in range(STEPS):
        own_down, halo_down = pltpu.roll(own, 1, 0), pltpu.roll(halo, 1, 0)
        own_up, halo_up = pltpu.roll(own, 7, 0), pltpu.roll(halo, 7, 0)
        own_sum = jnp.where(first, halo_down, own_down) + jnp.where(last, halo_up, own_up)
        halo_sum = jnp.where(first, own_down, halo_down) + jnp.where(last, own_up, halo_up)
        own_sum += pltpu.roll(own, 1, 1) + pltpu.roll(own, LANES - 1, 1)
        halo_sum += pltpu.roll(halo, 1, 1) + pltpu.roll(halo, LANES - 1, 1)
        own = keep_own * own + coef_own * own_sum
        halo = keep_halo * halo + coef_halo * halo_sum
    return own


def kernel(
    ty_num, tx_num, ens, coef, vertical, weights, pack, inc_ref, back_ref,
    tiles, edge_rows, strips, strips_in, field, strip_field, field_in, strip_field_in,
    got, out_rows, cur, cur_strip, fm, fe,
    local_sem, ens_send, ens_recv, obs_send, obs_recv, fld_send, fld_recv,
    sfl_send, sfl_recv, row_send, row_recv, str_send, str_recv, ret_send, ret_recv,
):
    f32 = jnp.float32
    levels = tiles.shape[1]
    groups = tx_num * GROUP // LANES
    per = levels // CHUNKS
    row, col = lax.axis_index("ty"), lax.axis_index("tx")

    def exists(move):
        down, right = move
        ok = None
        for shift, here, num in ((down, row, ty_num), (right, col, tx_num)):
            if shift:
                inside = here > 0 if shift < 0 else here < num - 1
                ok = inside if ok is None else jnp.logical_and(ok, inside)
        return ok

    def peer(move):
        return (row + move[0], col + move[1])

    barrier = pltpu.get_barrier_semaphore()

    @pl.loop(1, tx_num)
    def _(i):
        pl.semaphore_signal(
            barrier, inc=1, device_id=(row, lax.rem(col + i, tx_num)), device_id_type=MESH
        )

    for move in DIRS:
        if move[0]:
            @pl.when(exists(move))
            def _():
                pl.semaphore_signal(barrier, inc=1, device_id=peer(move), device_id_type=MESH)

    mine = pltpu.make_async_copy(
        ens.at[0, :, :, pl.ds(pl.multiple_of(col * LANES, LANES), LANES)],
        tiles.at[col], local_sem.at[0],
    )
    mine.start()
    mine_pack = pltpu.make_async_copy(pack.at[col], got.at[col], local_sem.at[1])
    mine_pack.start()

    lane = lax.broadcasted_iota(jnp.int32, (8, LANES), 1)
    sub = lax.broadcasted_iota(jnp.int32, (8, LANES), 0)
    low_half = lax.rem(lane, GROUP) < GROUP // 2
    upper = sub < HALO
    first, last = sub == 0, sub == 7

    def strip_of(tile):
        out = jnp.where(lane < GROUP, pltpu.roll(tile, GROUP // 2, 1), 0.0)
        for width in (16, 32, 64):
            out = out + pltpu.roll(out, width, 1)
        return out

    field[levels] = coef[...]
    strip_field[levels] = strip_of(coef[...])

    for i, move in enumerate(DIRS):
        @pl.when(jnp.logical_not(exists(move)))
        def _():
            strip_field_in[i] = jnp.zeros(strip_field_in.shape[1:], f32)
            strips_in[i] = jnp.zeros(strips_in.shape[1:], jnp.bfloat16)
        if move == DIRS[UP] or move == DIRS[DOWN]:
            @pl.when(jnp.logical_not(exists(move)))
            def _():
                field_in[int(i == DOWN)] = jnp.zeros(field_in.shape[1:], f32)
                rows = pl.ds(HALO * int(i == UP), HALO)
                edge_rows[:, :, rows] = jnp.zeros((tx_num, levels, HALO, LANES), jnp.bfloat16)

    awaited = tx_num - 1
    for move in DIRS:
        if move[0]:
            awaited = awaited + jnp.where(exists(move), 1, 0)
    pl.semaphore_wait(barrier, awaited)

    def obs_copy(to):
        return pltpu.make_async_remote_copy(
            src_ref=pack.at[to], dst_ref=got.at[col], send_sem=obs_send, recv_sem=obs_recv,
            device_id=(row, to), device_id_type=MESH,
        )

    def ens_copy(to, chunk):
        return pltpu.make_async_remote_copy(
            src_ref=ens.at[0, pl.ds(chunk * per, per), :, pl.ds(pl.multiple_of(to * LANES, LANES), LANES)],
            dst_ref=tiles.at[col, pl.ds(chunk * per, per)],
            send_sem=ens_send.at[chunk], recv_sem=ens_recv.at[chunk],
            device_id=(row, to), device_id_type=MESH,
        )

    def order(i):
        half = lax.div(i + 1, 2)
        return lax.rem(col + jnp.where(lax.rem(i, 2) == 1, half, tx_num - half), tx_num)

    @pl.loop(1, tx_num)
    def _(i):
        obs_copy(order(i)).start()

    for chunk in range(CHUNKS):
        @pl.loop(1, tx_num)
        def _(i):
            ens_copy(order(i), chunk).start()

    mine_pack.wait()
    others = pl.ds(0, tx_num - 1)
    pltpu.make_async_remote_copy(
        src_ref=pack.at[others], dst_ref=got.at[others], send_sem=obs_send, recv_sem=obs_recv,
        device_id=(row, col), device_id_type=MESH,
    ).wait_recv()
    slots = got[:, 0, :]
    wide_lane = lax.broadcasted_iota(jnp.int32, (tx_num, LANES), 1)
    level_row, column, value = [], [], []
    for j in range(8):
        cell = jnp.broadcast_to(slots[:, 8 + j : 9 + j], (tx_num, LANES)).astype(jnp.int32)
        level_row.append(jnp.where((cell >> 7) == wide_lane, 1.0, 0.0).astype(f32))
        column.append((cell & 127) == wide_lane)
        value.append(jnp.where(column[-1], jnp.broadcast_to(slots[:, j : j + 1], (tx_num, LANES)), 0.0))
    pick = jnp.concatenate(level_row, axis=0)
    spread = jnp.concatenate(split3(jnp.concatenate(value, axis=0)), axis=1)
    summed = jnp.dot(
        jnp.transpose(pick).astype(jnp.bfloat16), spread, preferred_element_type=f32
    )
    forcing = summed[:, :LANES] + summed[:, LANES : 2 * LANES] + summed[:, 2 * LANES :]
    for l in range(levels):
        tile = forcing[8 * l : 8 * l + 8]
        field[l] = tile
        strip_field[l] = strip_of(tile)

    def field_copy(i):
        side = int(i == DOWN)
        return pltpu.make_async_remote_copy(
            src_ref=field, dst_ref=field_in.at[1 - side],
            send_sem=fld_send.at[side], recv_sem=fld_recv.at[1 - side],
            device_id=peer(DIRS[i]), device_id_type=MESH,
        )

    def strip_field_copy(i):
        return pltpu.make_async_remote_copy(
            src_ref=strip_field, dst_ref=strip_field_in.at[7 - i],
            send_sem=sfl_send.at[i], recv_sem=sfl_recv.at[7 - i],
            device_id=peer(DIRS[i]), device_id_type=MESH,
        )

    def rows_copy(i, chunk):
        side = int(i == DOWN)
        cut = (slice(None), pl.ds(chunk * per, per), pl.ds(HALO * side, HALO))
        return pltpu.make_async_remote_copy(
            src_ref=tiles.at[cut], dst_ref=edge_rows.at[cut],
            send_sem=row_send.at[chunk, side], recv_sem=row_recv.at[chunk, 1 - side],
            device_id=peer(DIRS[i]), device_id_type=MESH,
        )

    def strip_copy(i, chunk):
        cut = pl.ds(chunk * per, per)
        return pltpu.make_async_remote_copy(
            src_ref=strips.at[cut], dst_ref=strips_in.at[7 - i, cut],
            send_sem=str_send.at[chunk, i], recv_sem=str_recv.at[chunk, 7 - i],
            device_id=peer(DIRS[i]), device_id_type=MESH,
        )

    for i, move in enumerate(DIRS):
        @pl.when(exists(move))
        def _():
            strip_field_copy(i).start()
            if i in (UP, DOWN):
                field_copy(i).start()

    def arrived(copy_of, i):
        copy_of(7 - i).wait_recv()

    for i, move in enumerate(DIRS):
        @pl.when(exists(move))
        def _():
            arrived(strip_field_copy, i)
            if i in (UP, DOWN):
                arrived(field_copy, i)

    def joined(here, there):
        return jnp.where(low_half, here, there)

    for l in range(levels + 1):
        fm[0, l] = field[l]
        fm[1, l] = jnp.where(upper, field_in[1, l], field_in[0, l])
        around = [strip_field_in[i, l] for i in range(8)]
        here = strip_field[l]
        fe[0, 0, l] = joined(here, around[4])
        fe[0, 1, l] = jnp.where(upper, joined(around[6], around[7]), joined(around[1], around[2]))
        fe[1, 0, l] = joined(around[3], here)
        fe[1, 1, l] = jnp.where(upper, joined(around[5], around[6]), joined(around[0], around[1]))

    mine.wait()
    for chunk in range(CHUNKS):
        cut = pl.ds(chunk * per, per)
        pltpu.make_async_remote_copy(
            src_ref=tiles.at[others, cut], dst_ref=tiles.at[others, cut],
            send_sem=ens_send.at[chunk], recv_sem=ens_recv.at[chunk],
            device_id=(row, col), device_id_type=MESH,
        ).wait_recv()
        for i in (UP, DOWN):
            @pl.when(exists(DIRS[i]))
            def _():
                rows_copy(i, chunk).start()

        @pl.loop(0, groups)
        def _(g):
            for l in range(chunk * per, (chunk + 1) * per):
                out = jnp.zeros((8, LANES), f32)
                for n in range(8):
                    tile = tiles[g * 8 + n, l].astype(f32)
                    turned = pltpu.roll(tile, (GROUP // 2 + GROUP * n) % LANES, 1)
                    out = jnp.where(lax.div(lane, GROUP) == n, turned, out)
                strips[l, g] = out.astype(jnp.bfloat16)

        for i, move in enumerate(DIRS):
            @pl.when(exists(move))
            def _():
                strip_copy(i, chunk).start()
        for i in (UP, DOWN):
            @pl.when(exists(DIRS[i]))
            def _():
                arrived(functools.partial(rows_copy, chunk=chunk), i)

        coef_own, coef_halo = fm[0, levels], fm[1, levels]
        keep_own, keep_halo = 1.0 - 4.0 * coef_own, 1.0 - 4.0 * coef_halo

        @pl.loop(0, tx_num)
        def _(k):
            for l in range(chunk * per, (chunk + 1) * per):
                own = tiles[k, l].astype(f32) * fm[0, l]
                halo = edge_rows[k, l].astype(f32) * fm[1, l]
                cur[k, l] = diffused(
                    own, halo, coef_own, coef_halo, keep_own, keep_halo, first, last
                )

        for i, move in enumerate(DIRS):
            @pl.when(exists(move))
            def _():
                arrived(functools.partial(strip_copy, chunk=chunk), i)

        @pl.loop(0, groups)
        def _(g):
            for l in range(chunk * per, (chunk + 1) * per):
                here = strips[l, g].astype(f32)
                around = [strips_in[i, l, g].astype(f32) for i in range(8)]
                sides = []
                for side in range(2):
                    if side == 0:
                        own = joined(here, around[4])
                        halo = jnp.where(
                            upper, joined(around[6], around[7]), joined(around[1], around[2])
                        )
                    else:
                        own = joined(around[3], here)
                        halo = jnp.where(
                            upper, joined(around[5], around[6]), joined(around[0], around[1])
                        )
                    c_own, c_halo = fe[side, 0, levels], fe[side, 1, levels]
                    sides.append(
                        diffused(
                            own * fe[side, 0, l], halo * fe[side, 1, l], c_own, c_halo,
                            1.0 - 4.0 * c_own, 1.0 - 4.0 * c_halo, first, last,
                        )
                    )
                cur_strip[g, l] = joined(sides[0], sides[1])

    def mixed(parts, l):
        total = None
        for m in range(max(0, l - 2), min(levels, l + 3)):
            term = vertical[l, m] * parts[m]
            total = term if total is None else total + term
        return total

    def add_member(k, sums):
        parts = [cur[k, m] for m in range(levels)]
        return tuple(
            sums[l] + (weights[k] * tiles[k, l].astype(f32)) * mixed(parts, l)
            for l in range(levels)
        )

    def add_group(g, sums):
        parts = [cur_strip[g, m] for m in range(levels)]
        scale = jnp.zeros((8, LANES), f32)
        for n in range(8):
            scale = jnp.where(lax.div(lane, GROUP) == n, weights[g * 8 + n], scale)
        return tuple(
            sums[l] + (scale * strips[l, g].astype(f32)) * mixed(parts, l) for l in range(levels)
        )

    zeros = tuple(jnp.zeros((8, LANES), f32) for _ in range(levels))
    main = lax.fori_loop(0, tx_num, add_member, zeros)
    side = lax.fori_loop(0, groups, add_group, zeros)
    increment = []
    for l in range(levels):
        edge = side[l]
        for width in (64, 32, 16):
            edge = edge + pltpu.roll(edge, width, 1)
        edge = pltpu.roll(edge, LANES - GROUP // 2, 1)
        increment.append(jnp.where((lane < HALO) | (lane >= LANES - HALO), edge, main[l]))
        inc_ref[l] = increment[-1]

    source = jnp.concatenate(increment + [jnp.zeros((LANES - 8 * levels, LANES), f32)], axis=0)
    taken = jnp.dot(
        pick.astype(jnp.bfloat16), jnp.concatenate(split3(source), axis=1),
        preferred_element_type=f32,
    )
    taken = taken[:, :LANES] + taken[:, LANES : 2 * LANES] + taken[:, 2 * LANES :]
    answer = jnp.zeros((tx_num, LANES), f32)
    for j in range(8):
        part = jnp.where(column[j], taken[tx_num * j : tx_num * (j + 1)], 0.0)
        answer = jnp.where(wide_lane == j, jnp.sum(part, axis=1, keepdims=True), answer)
    out_rows[:, 0, :] = answer

    def back_copy(to):
        return pltpu.make_async_remote_copy(
            src_ref=out_rows.at[to], dst_ref=back_ref.at[col],
            send_sem=ret_send, recv_sem=ret_recv, device_id=(row, to), device_id_type=MESH,
        )

    mine_back = pltpu.make_async_copy(out_rows.at[col], back_ref.at[col], local_sem.at[2])
    mine_back.start()

    @pl.loop(1, tx_num)
    def _(i):
        back_copy(order(i)).start()

    pltpu.make_async_remote_copy(
        src_ref=pack.at[others], dst_ref=got.at[others], send_sem=obs_send, recv_sem=obs_recv,
        device_id=(row, col), device_id_type=MESH,
    ).wait_send()
    for chunk in range(CHUNKS):
        cut = pl.ds(chunk * per, per)
        pltpu.make_async_remote_copy(
            src_ref=tiles.at[others, cut], dst_ref=tiles.at[others, cut],
            send_sem=ens_send.at[chunk], recv_sem=ens_recv.at[chunk],
            device_id=(row, col), device_id_type=MESH,
        ).wait_send()
    for i, move in enumerate(DIRS):
        @pl.when(exists(move))
        def _():
            strip_field_copy(i).wait_send()
            for chunk in range(CHUNKS):
                strip_copy(i, chunk).wait_send()
            if i in (UP, DOWN):
                field_copy(i).wait_send()
                for chunk in range(CHUNKS):
                    rows_copy(i, chunk).wait_send()
    mine_back.wait()
    pltpu.make_async_remote_copy(
        src_ref=out_rows.at[others], dst_ref=back_ref.at[others],
        send_sem=ret_send, recv_sem=ret_recv, device_id=(row, col), device_id_type=MESH,
    ).wait()


def shards(ty_num, tx_num, ensemble, diffusivity, vertical, weights, obs_value, obs_cell, obs_count):
    levels = ensemble.shape[1]
    slots = obs_value.shape[2]
    live = jnp.arange(slots, dtype=jnp.int32) < obs_count[0][:, None]
    cells = jnp.where(live, obs_cell[0], -1).astype(jnp.float32)
    pack = jnp.concatenate(
        [obs_value[0], cells, jnp.zeros((tx_num, LANES - 2 * slots), jnp.float32)], axis=1
    )[:, None, :]
    groups = tx_num * GROUP // LANES
    f32, bf16, dma = jnp.float32, jnp.bfloat16, pltpu.SemaphoreType.DMA
    vmem = pl.BlockSpec(memory_space=pltpu.VMEM)
    smem = pl.BlockSpec(memory_space=pltpu.SMEM)
    increment, back = pl.pallas_call(
        functools.partial(kernel, ty_num, tx_num),
        out_shape=(
            jax.ShapeDtypeStruct((levels, 8, LANES), f32),
            jax.ShapeDtypeStruct((tx_num, 1, LANES), f32),
        ),
        in_specs=[pl.BlockSpec(memory_space=pl.ANY), vmem, smem, smem, vmem],
        out_specs=(vmem, vmem),
        scratch_shapes=[
            pltpu.VMEM((tx_num, levels, 8, LANES), bf16),
            pltpu.VMEM((tx_num, levels, 8, LANES), bf16),
            pltpu.VMEM((levels, groups, 8, LANES), bf16),
            pltpu.VMEM((8, levels, groups, 8, LANES), bf16),
            pltpu.VMEM((levels + 1, 8, LANES), f32),
            pltpu.VMEM((levels + 1, 8, LANES), f32),
            pltpu.VMEM((2, levels + 1, 8, LANES), f32),
            pltpu.VMEM((8, levels + 1, 8, LANES), f32),
            pltpu.VMEM((tx_num, 1, LANES), f32),
            pltpu.VMEM((tx_num, 1, LANES), f32),
            pltpu.VMEM((tx_num, levels, 8, LANES), f32),
            pltpu.VMEM((groups, levels, 8, LANES), f32),
            pltpu.VMEM((2, levels + 1, 8, LANES), f32),
            pltpu.VMEM((2, 2, levels + 1, 8, LANES), f32),
            dma((3,)),
            dma((CHUNKS,)), dma((CHUNKS,)),
            dma, dma,
            dma((2,)), dma((2,)),
            dma((8,)), dma((8,)),
            dma((CHUNKS, 2)), dma((CHUNKS, 2)),
            dma((CHUNKS, 8)), dma((CHUNKS, 8)),
            dma, dma,
        ],
        compiler_params=pltpu.CompilerParams(collective_id=0, has_side_effects=True),
    )(ensemble, diffusivity, vertical, weights, pack)
    return increment, back[None, :, 0, :slots]


def solution(mesh):
    placed = (
        P("tx", None, "ty", None),
        P("ty", "tx"),
        P(),
        P(),
        P(("ty", "tx"), None, None),
        P(("ty", "tx"), None, None),
        P(("ty", "tx"), None),
    )
    return jax.shard_map(
        functools.partial(shards, mesh.shape["ty"], mesh.shape["tx"]),
        mesh=mesh,
        in_specs=placed,
        out_specs=(P(None, "ty", "tx"), P(("ty", "tx"), None, None)),
        check_vma=False,
    )
```

```python
import functools

import jax
import jax.numpy as jnp
from jax import lax
from jax.experimental import pallas as pl
from jax.experimental.pallas import tpu as pltpu
from jax.sharding import PartitionSpec as P

STEPS = 4
HALO = 4
LANES = 128
GROUP = 16
CHUNKS = 2
MESH = pl.DeviceIdType.MESH
DIRS = ((-1, -1), (-1, 0), (-1, 1), (0, -1), (0, 1), (1, -1), (1, 0), (1, 1))
UP, DOWN = 1, 6
PLACE = (3, 2, 4, 0, 1, 3, 2, 4)


def split3(x):
    hi = x.astype(jnp.bfloat16)
    rest = x - hi.astype(jnp.float32)
    mid = rest.astype(jnp.bfloat16)
    low = (rest - mid.astype(jnp.float32)).astype(jnp.bfloat16)
    return hi, mid, low


def diffused(rows, coef, keep):
    width = len(rows)
    for step in range(1, STEPS + 1):
        fresh = [None] * width
        for i in range(step, width - step):
            beside = pltpu.roll(rows[i], 1, 2) + pltpu.roll(rows[i], LANES - 1, 2)
            fresh[i] = keep(i) * rows[i] + coef(i) * (beside + (rows[i - 1] + rows[i + 1]))
        rows = fresh
    return rows[STEPS : width - STEPS]


def kernel(
    ty_num, tx_num, ens, coef, vertical, weights, pack, inc_ref, back_ref,
    tiles, turned, edge_rows, strips, strips_in, field, strip_field, field_in, strip_field_in,
    got, out_rows, cur, cur_strip, spread_field, spread_strip, scale, stage, edge_sum,
    local_sem, ens_send, ens_recv, obs_send, obs_recv, fld_send, fld_recv,
    sfl_send, sfl_recv, row_send, row_recv, str_send, str_recv, ret_send, ret_recv,
):
    f32 = jnp.float32
    levels = tiles.shape[1]
    batch = min(16, tx_num)
    batches = tx_num // batch
    per = levels // CHUNKS
    row, col = lax.axis_index("ty"), lax.axis_index("tx")

    def exists(move):
        down, right = move
        ok = None
        for shift, here, num in ((down, row, ty_num), (right, col, tx_num)):
            if shift:
                inside = here > 0 if shift < 0 else here < num - 1
                ok = inside if ok is None else jnp.logical_and(ok, inside)
        return ok

    def kept_rows(i):
        return {-1: pl.ds(HALO, HALO), 0: pl.ds(0, 8), 1: pl.ds(0, HALO)}[DIRS[i][0]]

    def peer(move):
        return (row + move[0], col + move[1])

    barrier = pltpu.get_barrier_semaphore()

    @pl.loop(1, tx_num)
    def _(i):
        pl.semaphore_signal(
            barrier, inc=1, device_id=(row, lax.rem(col + i, tx_num)), device_id_type=MESH
        )

    for move in DIRS:
        if move[0]:
            @pl.when(exists(move))
            def _():
                pl.semaphore_signal(barrier, inc=1, device_id=peer(move), device_id_type=MESH)

    mine = pltpu.make_async_copy(
        ens.at[0, :, :, pl.ds(pl.multiple_of(col * LANES, LANES), LANES)],
        tiles.at[col], local_sem.at[0],
    )
    mine.start()
    mine_pack = pltpu.make_async_copy(pack.at[col], got.at[col], local_sem.at[1])
    mine_pack.start()

    lane = lax.broadcasted_iota(jnp.int32, (8, LANES), 1)
    low_half = lax.rem(lane, GROUP) < GROUP // 2

    def into_strip(strip, tile, l, lane):
        moved = pltpu.roll(tile, (GROUP // 2 + GROUP * l) % LANES, tile.ndim - 1)
        return jnp.where(lax.div(lane, GROUP) == l, moved, strip)

    def strip_of(tile):
        out = jnp.where(lane < GROUP, pltpu.roll(tile, GROUP // 2, 1), 0.0)
        for width in (16, 32, 64):
            out = out + pltpu.roll(out, width, 1)
        return out

    field[levels] = coef[...]
    strip_field[1] = strip_of(coef[...])
    for k in range(tx_num):
        scale[k : k + 1, :] = jnp.full((1, LANES), weights[k], f32)

    for i, move in enumerate(DIRS):
        @pl.when(jnp.logical_not(exists(move)))
        def _():
            rows = kept_rows(i)
            size = HALO if move[0] else 8
            strip_field_in[PLACE[i], :, rows] = jnp.zeros((2, size, LANES), f32)
            strips_in[PLACE[i], rows] = jnp.zeros((size, tx_num, LANES), jnp.bfloat16)
            if i in (UP, DOWN):
                field_in[:, rows] = jnp.zeros((levels + 1, size, LANES), f32)
                edge_rows[:, rows] = jnp.zeros((levels, size, tx_num, LANES), jnp.bfloat16)

    awaited = tx_num - 1
    for move in DIRS:
        if move[0]:
            awaited = awaited + jnp.where(exists(move), 1, 0)
    pl.semaphore_wait(barrier, awaited)

    def obs_copy(to):
        return pltpu.make_async_remote_copy(
            src_ref=pack.at[to], dst_ref=got.at[col], send_sem=obs_send, recv_sem=obs_recv,
            device_id=(row, to), device_id_type=MESH,
        )

    def ens_copy(to, chunk):
        return pltpu.make_async_remote_copy(
            src_ref=ens.at[0, pl.ds(chunk * per, per), :, pl.ds(pl.multiple_of(to * LANES, LANES), LANES)],
            dst_ref=tiles.at[col, pl.ds(chunk * per, per)],
            send_sem=ens_send.at[chunk], recv_sem=ens_recv.at[chunk],
            device_id=(row, to), device_id_type=MESH,
        )

    def order(i):
        half = lax.div(i + 1, 2)
        return lax.rem(col + jnp.where(lax.rem(i, 2) == 1, half, tx_num - half), tx_num)

    @pl.loop(1, tx_num)
    def _(i):
        obs_copy(order(i)).start()

    for chunk in range(CHUNKS):
        @pl.loop(1, tx_num)
        def _(i):
            ens_copy(order(i), chunk).start()

    mine_pack.wait()
    others = pl.ds(0, tx_num - 1)
    pltpu.make_async_remote_copy(
        src_ref=pack.at[others], dst_ref=got.at[others], send_sem=obs_send, recv_sem=obs_recv,
        device_id=(row, col), device_id_type=MESH,
    ).wait_recv()
    slots = got[:, 0, :]
    wide_lane = lax.broadcasted_iota(jnp.int32, (tx_num, LANES), 1)
    level_row, column, value = [], [], []
    for j in range(8):
        cell = jnp.broadcast_to(slots[:, 8 + j : 9 + j], (tx_num, LANES)).astype(jnp.int32)
        level_row.append(jnp.where((cell >> 7) == wide_lane, 1.0, 0.0).astype(f32))
        column.append((cell & 127) == wide_lane)
        value.append(jnp.where(column[-1], jnp.broadcast_to(slots[:, j : j + 1], (tx_num, LANES)), 0.0))
    pick = jnp.concatenate(level_row, axis=0)
    spread = jnp.concatenate(split3(jnp.concatenate(value, axis=0)), axis=1)
    summed = jnp.dot(
        jnp.transpose(pick).astype(jnp.bfloat16), spread, preferred_element_type=f32
    )
    forcing = summed[:, :LANES] + summed[:, LANES : 2 * LANES] + summed[:, 2 * LANES :]
    strip = jnp.zeros((8, LANES), f32)
    for l in range(levels):
        tile = forcing[8 * l : 8 * l + 8]
        field[l] = tile
        strip = into_strip(strip, tile, l, lane)
    strip_field[0] = strip

    def field_copy(i):
        rows = kept_rows(7 - i)
        return pltpu.make_async_remote_copy(
            src_ref=field.at[:, rows], dst_ref=field_in.at[:, rows],
            send_sem=fld_send.at[i], recv_sem=fld_recv.at[7 - i],
            device_id=peer(DIRS[i]), device_id_type=MESH,
        )

    def strip_field_copy(i):
        rows = kept_rows(7 - i)
        return pltpu.make_async_remote_copy(
            src_ref=strip_field.at[:, rows], dst_ref=strip_field_in.at[PLACE[7 - i], :, rows],
            send_sem=sfl_send.at[i], recv_sem=sfl_recv.at[7 - i],
            device_id=peer(DIRS[i]), device_id_type=MESH,
        )

    def rows_copy(i, chunk):
        cut = (pl.ds(chunk * per, per), kept_rows(7 - i))
        return pltpu.make_async_remote_copy(
            src_ref=turned.at[cut], dst_ref=edge_rows.at[cut],
            send_sem=row_send.at[chunk, i], recv_sem=row_recv.at[chunk, 7 - i],
            device_id=peer(DIRS[i]), device_id_type=MESH,
        )

    def strip_copy(i):
        rows = kept_rows(7 - i)
        return pltpu.make_async_remote_copy(
            src_ref=strips.at[rows], dst_ref=strips_in.at[PLACE[7 - i], rows],
            send_sem=str_send.at[i], recv_sem=str_recv.at[7 - i],
            device_id=peer(DIRS[i]), device_id_type=MESH,
        )

    for i, move in enumerate(DIRS):
        @pl.when(exists(move))
        def _():
            strip_field_copy(i).start()
            if i in (UP, DOWN):
                field_copy(i).start()

    def arrived(copy_of, i):
        copy_of(7 - i).wait_recv()

    def edges(here, around, half):
        def joined(one, other):
            return jnp.where(half, one, other)

        return (
            (joined(here, around[1]), joined(around[2], around[4])),
            (joined(around[0], here), joined(around[3], around[2])),
        )

    def tall(i):
        return (0, i - HALO) if HALO <= i < HALO + 8 else (1, (i + HALO) % 8)

    def spread_rows(own, halo):
        pair = (own, halo)
        out = []
        for i in range(8 + 2 * HALO):
            which, r = tall(i)
            out.append(jnp.broadcast_to(pair[which][r : r + 1], (8, LANES)))
        return out

    def finish_fields():
        for i, move in enumerate(DIRS):
            @pl.when(exists(move))
            def _():
                arrived(strip_field_copy, i)
                if i in (UP, DOWN):
                    arrived(field_copy, i)
        for l in range(levels + 1):
            for i, line in enumerate(spread_rows(field[l], field_in[l])):
                spread_field[l, i] = line
                if l == levels:
                    spread_field[levels + 1, i] = 1.0 - 4.0 * line
        for kind in range(2):
            both = edges(strip_field[kind], [strip_field_in[i, kind] for i in range(5)], low_half)
            for side in range(2):
                for i, line in enumerate(spread_rows(*both[side])):
                    spread_strip[side, kind, i] = line
                    if kind == 1:
                        spread_strip[side, 2, i] = 1.0 - 4.0 * line

    def block(value):
        return value.astype(f32).reshape(batch // 8, 8, LANES)

    def members(b):
        return pl.ds(pl.multiple_of(b * batch, batch), batch)

    def share(chunk):
        cut = pl.ds(chunk * per, per)
        pltpu.make_async_remote_copy(
            src_ref=tiles.at[others, cut], dst_ref=tiles.at[others, cut],
            send_sem=ens_send.at[chunk], recv_sem=ens_recv.at[chunk],
            device_id=(row, col), device_id_type=MESH,
        ).wait_recv()

        @pl.loop(0, batches)
        def _(b):
            for l in range(chunk * per, (chunk + 1) * per):
                slot = l % 2
                stage[slot] = tiles[members(b), l].astype(f32).reshape(batch * 8, LANES)
                for r in range(8):
                    turned[l, r, members(b)] = stage[slot, pl.ds(r, batch, stride=8)].astype(jnp.bfloat16)

        for i in (UP, DOWN):
            @pl.when(exists(DIRS[i]))
            def _():
                rows_copy(i, chunk).start()

    wide = lax.broadcasted_iota(jnp.int32, (batch // 8, 8, LANES), 2)

    def share_strips():
        @pl.loop(0, batches)
        def _(b):
            for r in range(8):
                out = jnp.zeros((batch // 8, 8, LANES), f32)
                for l in range(levels):
                    out = into_strip(out, block(turned[l, r, members(b)]), l, wide)
                strips[r, members(b)] = out.reshape(batch, LANES).astype(jnp.bfloat16)

        for i, move in enumerate(DIRS):
            @pl.when(exists(move))
            def _():
                strip_copy(i).start()

    def diffuse_main(chunk):
        for i in (UP, DOWN):
            @pl.when(exists(DIRS[i]))
            def _():
                arrived(functools.partial(rows_copy, chunk=chunk), i)

        @pl.loop(0, batches)
        def _(b):
            @pl.loop(chunk * per, (chunk + 1) * per)
            def _(l):
                rows = []
                for i in range(8 + 2 * HALO):
                    which, r = tall(i)
                    here = (turned, edge_rows)[which][l, r, members(b)]
                    rows.append(block(here) * spread_field[l, i])
                done = diffused(
                    rows, lambda i: spread_field[levels, i], lambda i: spread_field[levels + 1, i]
                )
                for r in range(8):
                    cur[l, r, members(b)] = done[r].reshape(batch, LANES)

    def diffuse_edges():
        for i, move in enumerate(DIRS):
            @pl.when(exists(move))
            def _():
                arrived(strip_copy, i)
        half = lax.rem(wide, GROUP) < GROUP // 2

        @pl.loop(0, batches)
        def _(b):
            results = []
            for side in range(2):
                rows = []
                for i in range(8 + 2 * HALO):
                    which, r = tall(i)
                    here = block(strips[r, members(b)])
                    around = [block(strips_in[n, r, members(b)]) for n in range(5)]
                    rows.append(edges(here, around, half)[side][which] * spread_strip[side, 0, i])
                results.append(
                    diffused(
                        rows, lambda i: spread_strip[side, 1, i], lambda i: spread_strip[side, 2, i]
                    )
                )
            for r in range(8):
                both = jnp.where(half, results[0][r], results[1][r])
                cur_strip[r, members(b)] = both.reshape(batch, LANES)

    mine.wait()
    share(0)
    finish_fields()
    for chunk in range(1, CHUNKS):
        share(chunk)
    share_strips()
    for chunk in range(CHUNKS):
        diffuse_main(chunk)
    diffuse_edges()

    band = []
    for shift in range(-2, 3):
        line = jnp.zeros((8, LANES), f32)
        for l in range(max(0, -shift), min(levels, levels - shift)):
            line = jnp.where(lax.div(lane, GROUP) == l, vertical[l, l + shift], line)
        band.append(line)

    def mixed(parts, l):
        total = None
        for m in range(max(0, l - 2), min(levels, l + 3)):
            term = vertical[l, m] * parts[m]
            total = term if total is None else total + term
        return total

    def folded(total):
        return jnp.sum(jnp.sum(total, axis=0), axis=0, keepdims=True)

    @pl.loop(0, 8)
    def _(r):
        sums = [jnp.zeros((batch // 8, 8, LANES), f32)] * levels
        side = jnp.zeros((batch // 8, 8, LANES), f32)
        for b in range(batches):
            some = pl.ds(b * batch, batch)
            factor = block(scale[some])
            parts = [block(cur[m, r, some]) for m in range(levels)]
            for l in range(levels):
                sums[l] = sums[l] + (factor * block(turned[l, r, some])) * mixed(parts, l)
            part = block(cur_strip[r, some])
            total = jnp.zeros((batch // 8, 8, LANES), f32)
            for shift in range(-2, 3):
                total = total + band[shift + 2] * pltpu.roll(part, (-GROUP * shift) % LANES, 2)
            side = side + (factor * block(strips[r, some])) * total
        for l in range(levels):
            inc_ref[l, pl.ds(r, 1)] = folded(sums[l])
        edge_sum[pl.ds(r, 1)] = folded(side)

    increment = []
    for l in range(levels):
        edge = pltpu.roll(edge_sum[...], (LANES - GROUP // 2 - GROUP * l) % LANES, 1)
        increment.append(jnp.where((lane < HALO) | (lane >= LANES - HALO), edge, inc_ref[l]))
        inc_ref[l] = increment[-1]

    source = jnp.concatenate(increment + [jnp.zeros((LANES - 8 * levels, LANES), f32)], axis=0)
    taken = jnp.dot(
        pick.astype(jnp.bfloat16), jnp.concatenate(split3(source), axis=1),
        preferred_element_type=f32,
    )
    taken = taken[:, :LANES] + taken[:, LANES : 2 * LANES] + taken[:, 2 * LANES :]
    answer = jnp.zeros((tx_num, LANES), f32)
    for j in range(8):
        part = jnp.where(column[j], taken[tx_num * j : tx_num * (j + 1)], 0.0)
        answer = jnp.where(wide_lane == j, jnp.sum(part, axis=1, keepdims=True), answer)
    out_rows[:, 0, :] = answer

    def back_copy(to):
        return pltpu.make_async_remote_copy(
            src_ref=out_rows.at[to], dst_ref=back_ref.at[col],
            send_sem=ret_send, recv_sem=ret_recv, device_id=(row, to), device_id_type=MESH,
        )

    mine_back = pltpu.make_async_copy(out_rows.at[col], back_ref.at[col], local_sem.at[2])
    mine_back.start()

    @pl.loop(1, tx_num)
    def _(i):
        back_copy(order(i)).start()

    pltpu.make_async_remote_copy(
        src_ref=pack.at[others], dst_ref=got.at[others], send_sem=obs_send, recv_sem=obs_recv,
        device_id=(row, col), device_id_type=MESH,
    ).wait_send()
    for chunk in range(CHUNKS):
        cut = pl.ds(chunk * per, per)
        pltpu.make_async_remote_copy(
            src_ref=tiles.at[others, cut], dst_ref=tiles.at[others, cut],
            send_sem=ens_send.at[chunk], recv_sem=ens_recv.at[chunk],
            device_id=(row, col), device_id_type=MESH,
        ).wait_send()
    for i, move in enumerate(DIRS):
        @pl.when(exists(move))
        def _():
            strip_field_copy(i).wait_send()
            strip_copy(i).wait_send()
            if i in (UP, DOWN):
                field_copy(i).wait_send()
                for chunk in range(CHUNKS):
                    rows_copy(i, chunk).wait_send()
    mine_back.wait()
    pltpu.make_async_remote_copy(
        src_ref=out_rows.at[others], dst_ref=back_ref.at[others],
        send_sem=ret_send, recv_sem=ret_recv, device_id=(row, col), device_id_type=MESH,
    ).wait()


def shards(ty_num, tx_num, ensemble, diffusivity, vertical, weights, obs_value, obs_cell, obs_count):
    levels = ensemble.shape[1]
    slots = obs_value.shape[2]
    live = jnp.arange(slots, dtype=jnp.int32) < obs_count[0][:, None]
    cells = jnp.where(live, obs_cell[0], -1).astype(jnp.float32)
    pack = jnp.concatenate(
        [obs_value[0], cells, jnp.zeros((tx_num, LANES - 2 * slots), jnp.float32)], axis=1
    )[:, None, :]
    batch = min(16, tx_num)
    f32, bf16, dma = jnp.float32, jnp.bfloat16, pltpu.SemaphoreType.DMA
    vmem = pl.BlockSpec(memory_space=pltpu.VMEM)
    smem = pl.BlockSpec(memory_space=pltpu.SMEM)
    increment, back = pl.pallas_call(
        functools.partial(kernel, ty_num, tx_num),
        out_shape=(
            jax.ShapeDtypeStruct((levels, 8, LANES), f32),
            jax.ShapeDtypeStruct((tx_num, 1, LANES), f32),
        ),
        in_specs=[pl.BlockSpec(memory_space=pl.ANY), vmem, smem, smem, vmem],
        out_specs=(vmem, vmem),
        scratch_shapes=[
            pltpu.VMEM((tx_num, levels, 8, LANES), bf16),
            pltpu.VMEM((levels, 8, tx_num, LANES), bf16),
            pltpu.VMEM((levels, 8, tx_num, LANES), bf16),
            pltpu.VMEM((8, tx_num, LANES), bf16),
            pltpu.VMEM((5, 8, tx_num, LANES), bf16),
            pltpu.VMEM((levels + 1, 8, LANES), f32),
            pltpu.VMEM((2, 8, LANES), f32),
            pltpu.VMEM((levels + 1, 8, LANES), f32),
            pltpu.VMEM((5, 2, 8, LANES), f32),
            pltpu.VMEM((tx_num, 1, LANES), f32),
            pltpu.VMEM((tx_num, 1, LANES), f32),
            pltpu.VMEM((levels, 8, tx_num, LANES), f32),
            pltpu.VMEM((8, tx_num, LANES), f32),
            pltpu.VMEM((levels + 2, 8 + 2 * HALO, 8, LANES), f32),
            pltpu.VMEM((2, 3, 8 + 2 * HALO, 8, LANES), f32),
            pltpu.VMEM((tx_num, LANES), f32),
            pltpu.VMEM((2, batch * 8, LANES), f32),
            pltpu.VMEM((8, LANES), f32),
            dma((3,)),
            dma((CHUNKS,)), dma((CHUNKS,)),
            dma, dma,
            dma((8,)), dma((8,)),
            dma((8,)), dma((8,)),
            dma((CHUNKS, 8)), dma((CHUNKS, 8)),
            dma((8,)), dma((8,)),
            dma, dma,
        ],
        compiler_params=pltpu.CompilerParams(collective_id=0, has_side_effects=True),
    )(ensemble, diffusivity, vertical, weights, pack)
    return increment, back[None, :, 0, :slots]


def solution(mesh):
    placed = (
        P("tx", None, "ty", None),
        P("ty", "tx"),
        P(),
        P(),
        P(("ty", "tx"), None, None),
        P(("ty", "tx"), None, None),
        P(("ty", "tx"), None),
    )
    return jax.shard_map(
        functools.partial(shards, mesh.shape["ty"], mesh.shape["tx"]),
        mesh=mesh,
        in_specs=placed,
        out_specs=(P(None, "ty", "tx"), P(("ty", "tx"), None, None)),
        check_vma=False,
    )
```

```python
import functools

import jax
import jax.numpy as jnp
from jax import lax
from jax.experimental import pallas as pl
from jax.experimental.pallas import tpu as pltpu
from jax.sharding import PartitionSpec as P

STEPS = 4
HALO = 4
LANES = 128
GROUP = 16
CHUNKS = 2
MESH = pl.DeviceIdType.MESH
DIRS = ((-1, -1), (-1, 0), (-1, 1), (0, -1), (0, 1), (1, -1), (1, 0), (1, 1))
UP, DOWN = 1, 6
PLACE = (3, 2, 4, 0, 1, 3, 2, 4)


def split3(x):
    hi = x.astype(jnp.bfloat16)
    rest = x - hi.astype(jnp.float32)
    mid = rest.astype(jnp.bfloat16)
    low = (rest - mid.astype(jnp.float32)).astype(jnp.bfloat16)
    return hi, mid, low


def diffused(rows, coef, keep):
    width = len(rows)
    for step in range(1, STEPS + 1):
        fresh = [None] * width
        for i in range(step, width - step):
            beside = pltpu.roll(rows[i], 1, 2) + pltpu.roll(rows[i], LANES - 1, 2)
            fresh[i] = keep(i) * rows[i] + coef(i) * (beside + (rows[i - 1] + rows[i + 1]))
        rows = fresh
    return rows[STEPS : width - STEPS]


def kernel(
    ty_num, tx_num, ens, coef_in, vertical_in, weights_in, value_in, cell_in, count_in, inc_ref, back_ref,
    coef, vertical, weights, obs_value, obs_cell, obs_count, lines, pack,
    tiles, turned, edge_rows, strips, strips_in, field, strip_field, field_in, strip_field_in,
    got, out_rows, cur, cur_strip, spread_field, spread_strip, scale, stage, edge_sum,
    local_sem, ens_send, ens_recv, obs_send, obs_recv, fld_send, fld_recv,
    sfl_send, sfl_recv, row_send, row_recv, str_send, str_recv, ret_send, ret_recv,
):
    f32 = jnp.float32
    levels = tiles.shape[1]
    batch = min(16, tx_num)
    batches = tx_num // batch
    per = levels // CHUNKS
    row, col = lax.axis_index("ty"), lax.axis_index("tx")

    def exists(move):
        down, right = move
        ok = None
        for shift, here, num in ((down, row, ty_num), (right, col, tx_num)):
            if shift:
                inside = here > 0 if shift < 0 else here < num - 1
                ok = inside if ok is None else jnp.logical_and(ok, inside)
        return ok

    def kept_rows(i):
        return {-1: pl.ds(HALO, HALO), 0: pl.ds(0, 8), 1: pl.ds(0, HALO)}[DIRS[i][0]]

    def peer(move):
        return (row + move[0], col + move[1])

    barrier = pltpu.get_barrier_semaphore()

    @pl.loop(1, tx_num)
    def _(i):
        pl.semaphore_signal(
            barrier, inc=1, device_id=(row, lax.rem(col + i, tx_num)), device_id_type=MESH
        )

    for move in DIRS:
        if move[0]:
            @pl.when(exists(move))
            def _():
                pl.semaphore_signal(barrier, inc=1, device_id=peer(move), device_id_type=MESH)

    mine = pltpu.make_async_copy(
        ens.at[0, :, :, pl.ds(pl.multiple_of(col * LANES, LANES), LANES)],
        tiles.at[col], local_sem.at[0],
    )
    small = [
        pltpu.make_async_copy(source, target, local_sem.at[3 + n])
        for n, (source, target) in enumerate((
            (value_in, obs_value), (cell_in, obs_cell), (count_in, obs_count),
            (coef_in, coef), (vertical_in, vertical), (weights_in, weights),
        ))
    ]
    for copy in small:
        copy.start()
    mine.start()

    awaited = tx_num - 1
    for move in DIRS:
        if move[0]:
            awaited = awaited + jnp.where(exists(move), 1, 0)
    pl.semaphore_wait(barrier, awaited)

    def obs_copy(to):
        return pltpu.make_async_remote_copy(
            src_ref=pack.at[to], dst_ref=got.at[col], send_sem=obs_send, recv_sem=obs_recv,
            device_id=(row, to), device_id_type=MESH,
        )

    def ens_copy(to, chunk):
        return pltpu.make_async_remote_copy(
            src_ref=ens.at[0, pl.ds(chunk * per, per), :, pl.ds(pl.multiple_of(to * LANES, LANES), LANES)],
            dst_ref=tiles.at[col, pl.ds(chunk * per, per)],
            send_sem=ens_send.at[chunk], recv_sem=ens_recv.at[chunk],
            device_id=(row, to), device_id_type=MESH,
        )

    def order(i):
        half = lax.div(i + 1, 2)
        return lax.rem(col + jnp.where(lax.rem(i, 2) == 1, half, tx_num - half), tx_num)

    def send_ens(chunk):
        @pl.loop(1, tx_num)
        def _(i):
            ens_copy(order(i), chunk).start()

    send_ens(0)

    for copy in small:
        copy.wait()
    live = lax.broadcasted_iota(jnp.int32, (8, tx_num), 0) < jnp.broadcast_to(obs_count[...], (8, tx_num))
    lines[...] = jnp.zeros(lines.shape, f32)
    lines[0:8, 0:tx_num] = obs_value[0]
    lines[8:16, 0:tx_num] = jnp.where(live, obs_cell[0], -1).astype(f32)
    pack[:, 0, :] = jnp.transpose(lines[...])[0:tx_num]
    mine_pack = pltpu.make_async_copy(pack.at[col], got.at[col], local_sem.at[1])
    mine_pack.start()

    @pl.loop(1, tx_num)
    def _(i):
        obs_copy(order(i)).start()

    for chunk in range(1, CHUNKS):
        send_ens(chunk)

    lane = lax.broadcasted_iota(jnp.int32, (8, LANES), 1)
    low_half = lax.rem(lane, GROUP) < GROUP // 2

    def into_strip(strip, tile, l, lane):
        moved = pltpu.roll(tile, (GROUP // 2 + GROUP * l) % LANES, tile.ndim - 1)
        return jnp.where(lax.div(lane, GROUP) == l, moved, strip)

    def strip_of(tile):
        out = jnp.where(lane < GROUP, pltpu.roll(tile, GROUP // 2, 1), 0.0)
        for width in (16, 32, 64):
            out = out + pltpu.roll(out, width, 1)
        return out

    field[levels] = coef[...]
    strip_field[1] = strip_of(coef[...])
    for k in range(tx_num):
        scale[k : k + 1, :] = jnp.full((1, LANES), weights[k], f32)

    for i, move in enumerate(DIRS):
        @pl.when(jnp.logical_not(exists(move)))
        def _():
            rows = kept_rows(i)
            size = HALO if move[0] else 8
            strip_field_in[PLACE[i], :, rows] = jnp.zeros((2, size, LANES), f32)
            strips_in[PLACE[i], rows] = jnp.zeros((size, tx_num, LANES), jnp.bfloat16)
            if i in (UP, DOWN):
                field_in[:, rows] = jnp.zeros((levels + 1, size, LANES), f32)
                edge_rows[:, rows] = jnp.zeros((levels, size, tx_num, LANES), jnp.bfloat16)

    mine_pack.wait()
    others = pl.ds(0, tx_num - 1)
    pltpu.make_async_remote_copy(
        src_ref=pack.at[others], dst_ref=got.at[others], send_sem=obs_send, recv_sem=obs_recv,
        device_id=(row, col), device_id_type=MESH,
    ).wait_recv()
    slots = got[:, 0, :]
    wide_lane = lax.broadcasted_iota(jnp.int32, (tx_num, LANES), 1)
    level_row, column, value = [], [], []
    for j in range(8):
        cell = jnp.broadcast_to(slots[:, 8 + j : 9 + j], (tx_num, LANES)).astype(jnp.int32)
        level_row.append(jnp.where((cell >> 7) == wide_lane, 1.0, 0.0).astype(f32))
        column.append((cell & 127) == wide_lane)
        value.append(jnp.where(column[-1], jnp.broadcast_to(slots[:, j : j + 1], (tx_num, LANES)), 0.0))
    pick = jnp.concatenate(level_row, axis=0)
    spread = jnp.concatenate(split3(jnp.concatenate(value, axis=0)), axis=1)
    summed = jnp.dot(
        jnp.transpose(pick).astype(jnp.bfloat16), spread, preferred_element_type=f32
    )
    forcing = summed[:, :LANES] + summed[:, LANES : 2 * LANES] + summed[:, 2 * LANES :]
    strip = jnp.zeros((8, LANES), f32)
    for l in range(levels):
        tile = forcing[8 * l : 8 * l + 8]
        field[l] = tile
        strip = into_strip(strip, tile, l, lane)
    strip_field[0] = strip

    def field_copy(i):
        rows = kept_rows(7 - i)
        return pltpu.make_async_remote_copy(
            src_ref=field.at[:, rows], dst_ref=field_in.at[:, rows],
            send_sem=fld_send.at[i], recv_sem=fld_recv.at[7 - i],
            device_id=peer(DIRS[i]), device_id_type=MESH,
        )

    def strip_field_copy(i):
        rows = kept_rows(7 - i)
        return pltpu.make_async_remote_copy(
            src_ref=strip_field.at[:, rows], dst_ref=strip_field_in.at[PLACE[7 - i], :, rows],
            send_sem=sfl_send.at[i], recv_sem=sfl_recv.at[7 - i],
            device_id=peer(DIRS[i]), device_id_type=MESH,
        )

    def rows_copy(i, chunk):
        cut = (pl.ds(chunk * per, per), kept_rows(7 - i))
        return pltpu.make_async_remote_copy(
            src_ref=turned.at[cut], dst_ref=edge_rows.at[cut],
            send_sem=row_send.at[chunk, i], recv_sem=row_recv.at[chunk, 7 - i],
            device_id=peer(DIRS[i]), device_id_type=MESH,
        )

    def strip_copy(i):
        rows = kept_rows(7 - i)
        return pltpu.make_async_remote_copy(
            src_ref=strips.at[rows], dst_ref=strips_in.at[PLACE[7 - i], rows],
            send_sem=str_send.at[i], recv_sem=str_recv.at[7 - i],
            device_id=peer(DIRS[i]), device_id_type=MESH,
        )

    for i, move in enumerate(DIRS):
        @pl.when(exists(move))
        def _():
            strip_field_copy(i).start()
            if i in (UP, DOWN):
                field_copy(i).start()

    def arrived(copy_of, i):
        copy_of(7 - i).wait_recv()

    def edges(here, around, half):
        def joined(one, other):
            return jnp.where(half, one, other)

        return (
            (joined(here, around[1]), joined(around[2], around[4])),
            (joined(around[0], here), joined(around[3], around[2])),
        )

    def tall(i):
        return (0, i - HALO) if HALO <= i < HALO + 8 else (1, (i + HALO) % 8)

    def spread_rows(own, halo):
        pair = (own, halo)
        out = []
        for i in range(8 + 2 * HALO):
            which, r = tall(i)
            out.append(jnp.broadcast_to(pair[which][r : r + 1], (8, LANES)))
        return out

    def finish_fields():
        for i, move in enumerate(DIRS):
            @pl.when(exists(move))
            def _():
                arrived(strip_field_copy, i)
                if i in (UP, DOWN):
                    arrived(field_copy, i)
        for l in range(levels + 1):
            for i, line in enumerate(spread_rows(field[l], field_in[l])):
                spread_field[l, i] = line
                if l == levels:
                    spread_field[levels + 1, i] = 1.0 - 4.0 * line
        for kind in range(2):
            both = edges(strip_field[kind], [strip_field_in[i, kind] for i in range(5)], low_half)
            for side in range(2):
                for i, line in enumerate(spread_rows(*both[side])):
                    spread_strip[side, kind, i] = line
                    if kind == 1:
                        spread_strip[side, 2, i] = 1.0 - 4.0 * line

    def block(value):
        return value.astype(f32).reshape(batch // 8, 8, LANES)

    def members(b):
        return pl.ds(pl.multiple_of(b * batch, batch), batch)

    def share(chunk):
        cut = pl.ds(chunk * per, per)
        pltpu.make_async_remote_copy(
            src_ref=tiles.at[others, cut], dst_ref=tiles.at[others, cut],
            send_sem=ens_send.at[chunk], recv_sem=ens_recv.at[chunk],
            device_id=(row, col), device_id_type=MESH,
        ).wait_recv()

        @pl.loop(0, batches)
        def _(b):
            for l in range(chunk * per, (chunk + 1) * per):
                slot = l % 2
                stage[slot] = tiles[members(b), l].astype(f32).reshape(batch * 8, LANES)
                for r in range(8):
                    turned[l, r, members(b)] = stage[slot, pl.ds(r, batch, stride=8)].astype(jnp.bfloat16)

        for i in (UP, DOWN):
            @pl.when(exists(DIRS[i]))
            def _():
                rows_copy(i, chunk).start()

    wide = lax.broadcasted_iota(jnp.int32, (batch // 8, 8, LANES), 2)

    def share_strips():
        @pl.loop(0, batches)
        def _(b):
            for r in range(8):
                out = jnp.zeros((batch // 8, 8, LANES), f32)
                for l in range(levels):
                    out = into_strip(out, block(turned[l, r, members(b)]), l, wide)
                strips[r, members(b)] = out.reshape(batch, LANES).astype(jnp.bfloat16)

        for i, move in enumerate(DIRS):
            @pl.when(exists(move))
            def _():
                strip_copy(i).start()

    def diffuse_main(chunk):
        for i in (UP, DOWN):
            @pl.when(exists(DIRS[i]))
            def _():
                arrived(functools.partial(rows_copy, chunk=chunk), i)

        @pl.loop(0, batches)
        def _(b):
            @pl.loop(chunk * per, (chunk + 1) * per)
            def _(l):
                rows = []
                for i in range(8 + 2 * HALO):
                    which, r = tall(i)
                    here = (turned, edge_rows)[which][l, r, members(b)]
                    rows.append(block(here) * spread_field[l, i])
                done = diffused(
                    rows, lambda i: spread_field[levels, i], lambda i: spread_field[levels + 1, i]
                )
                for r in range(8):
                    cur[l, r, members(b)] = done[r].reshape(batch, LANES)

    def diffuse_edges():
        for i, move in enumerate(DIRS):
            @pl.when(exists(move))
            def _():
                arrived(strip_copy, i)
        half = lax.rem(wide, GROUP) < GROUP // 2

        @pl.loop(0, batches)
        def _(b):
            results = []
            for side in range(2):
                rows = []
                for i in range(8 + 2 * HALO):
                    which, r = tall(i)
                    here = block(strips[r, members(b)])
                    around = [block(strips_in[n, r, members(b)]) for n in range(5)]
                    rows.append(edges(here, around, half)[side][which] * spread_strip[side, 0, i])
                results.append(
                    diffused(
                        rows, lambda i: spread_strip[side, 1, i], lambda i: spread_strip[side, 2, i]
                    )
                )
            for r in range(8):
                both = jnp.where(half, results[0][r], results[1][r])
                cur_strip[r, members(b)] = both.reshape(batch, LANES)

    mine.wait()
    share(0)
    finish_fields()
    for chunk in range(1, CHUNKS):
        share(chunk)
    share_strips()
    for chunk in range(CHUNKS):
        diffuse_main(chunk)
    diffuse_edges()

    band = []
    for shift in range(-2, 3):
        line = jnp.zeros((8, LANES), f32)
        for l in range(max(0, -shift), min(levels, levels - shift)):
            line = jnp.where(lax.div(lane, GROUP) == l, vertical[l, l + shift], line)
        band.append(line)

    def mixed(parts, l):
        total = None
        for m in range(max(0, l - 2), min(levels, l + 3)):
            term = vertical[l, m] * parts[m]
            total = term if total is None else total + term
        return total

    def folded(total):
        return jnp.sum(jnp.sum(total, axis=0), axis=0, keepdims=True)

    @pl.loop(0, 8)
    def _(r):
        sums = [jnp.zeros((batch // 8, 8, LANES), f32)] * levels
        side = jnp.zeros((batch // 8, 8, LANES), f32)
        for b in range(batches):
            some = pl.ds(b * batch, batch)
            factor = block(scale[some])
            parts = [block(cur[m, r, some]) for m in range(levels)]
            for l in range(levels):
                sums[l] = sums[l] + (factor * block(turned[l, r, some])) * mixed(parts, l)
            part = block(cur_strip[r, some])
            total = jnp.zeros((batch // 8, 8, LANES), f32)
            for shift in range(-2, 3):
                total = total + band[shift + 2] * pltpu.roll(part, (-GROUP * shift) % LANES, 2)
            side = side + (factor * block(strips[r, some])) * total
        for l in range(levels):
            inc_ref[l, pl.ds(r, 1)] = folded(sums[l])
        edge_sum[pl.ds(r, 1)] = folded(side)

    increment = []
    for l in range(levels):
        edge = pltpu.roll(edge_sum[...], (LANES - GROUP // 2 - GROUP * l) % LANES, 1)
        increment.append(jnp.where((lane < HALO) | (lane >= LANES - HALO), edge, inc_ref[l]))
        inc_ref[l] = increment[-1]

    source = jnp.concatenate(increment + [jnp.zeros((LANES - 8 * levels, LANES), f32)], axis=0)
    taken = jnp.dot(
        pick.astype(jnp.bfloat16), jnp.concatenate(split3(source), axis=1),
        preferred_element_type=f32,
    )
    taken = taken[:, :LANES] + taken[:, LANES : 2 * LANES] + taken[:, 2 * LANES :]
    answer = jnp.zeros((tx_num, LANES), f32)
    for j in range(8):
        part = jnp.where(column[j], taken[tx_num * j : tx_num * (j + 1)], 0.0)
        answer = jnp.where(wide_lane == j, jnp.sum(part, axis=1, keepdims=True), answer)
    out_rows[:, 0, :] = answer

    def back_copy(to):
        return pltpu.make_async_remote_copy(
            src_ref=out_rows.at[to], dst_ref=back_ref.at[col],
            send_sem=ret_send, recv_sem=ret_recv, device_id=(row, to), device_id_type=MESH,
        )

    mine_back = pltpu.make_async_copy(out_rows.at[col], back_ref.at[col], local_sem.at[2])
    mine_back.start()

    @pl.loop(1, tx_num)
    def _(i):
        back_copy(order(i)).start()

    pltpu.make_async_remote_copy(
        src_ref=pack.at[others], dst_ref=got.at[others], send_sem=obs_send, recv_sem=obs_recv,
        device_id=(row, col), device_id_type=MESH,
    ).wait_send()
    for chunk in range(CHUNKS):
        cut = pl.ds(chunk * per, per)
        pltpu.make_async_remote_copy(
            src_ref=tiles.at[others, cut], dst_ref=tiles.at[others, cut],
            send_sem=ens_send.at[chunk], recv_sem=ens_recv.at[chunk],
            device_id=(row, col), device_id_type=MESH,
        ).wait_send()
    for i, move in enumerate(DIRS):
        @pl.when(exists(move))
        def _():
            strip_field_copy(i).wait_send()
            strip_copy(i).wait_send()
            if i in (UP, DOWN):
                field_copy(i).wait_send()
                for chunk in range(CHUNKS):
                    rows_copy(i, chunk).wait_send()
    mine_back.wait()
    pltpu.make_async_remote_copy(
        src_ref=out_rows.at[others], dst_ref=back_ref.at[others],
        send_sem=ret_send, recv_sem=ret_recv, device_id=(row, col), device_id_type=MESH,
    ).wait()


def hand_over(slots, inc_in, back_in, inc_out, back_out):
    inc_out[...] = inc_in[...]
    back_out[0] = jnp.transpose(back_in[:, 0, :])[:slots]


def shards(ty_num, tx_num, ensemble, diffusivity, vertical, weights, obs_value, obs_cell, obs_count):
    levels = ensemble.shape[1]
    slots = obs_value.shape[2]
    batch = min(16, tx_num)
    f32, bf16, dma = jnp.float32, jnp.bfloat16, pltpu.SemaphoreType.DMA
    vmem = pl.BlockSpec(memory_space=pltpu.VMEM)
    hbm = pl.BlockSpec(memory_space=pltpu.HBM)
    increment, back = pl.pallas_call(
        functools.partial(kernel, ty_num, tx_num),
        out_shape=(
            jax.ShapeDtypeStruct((levels, 8, LANES), f32),
            jax.ShapeDtypeStruct((tx_num, 1, LANES), f32),
        ),
        in_specs=[hbm] * 7,
        out_specs=(vmem, vmem),
        scratch_shapes=[
            pltpu.VMEM(diffusivity.shape, f32),
            pltpu.SMEM(vertical.shape, f32),
            pltpu.SMEM(weights.shape, f32),
            pltpu.VMEM((1, slots, tx_num), f32),
            pltpu.VMEM((1, slots, tx_num), jnp.int32),
            pltpu.VMEM(obs_count.shape, jnp.int32),
            pltpu.VMEM((LANES, LANES), f32),
            pltpu.VMEM((tx_num, 1, LANES), f32),
            pltpu.VMEM((tx_num, levels, 8, LANES), bf16),
            pltpu.VMEM((levels, 8, tx_num, LANES), bf16),
            pltpu.VMEM((levels, 8, tx_num, LANES), bf16),
            pltpu.VMEM((8, tx_num, LANES), bf16),
            pltpu.VMEM((5, 8, tx_num, LANES), bf16),
            pltpu.VMEM((levels + 1, 8, LANES), f32),
            pltpu.VMEM((2, 8, LANES), f32),
            pltpu.VMEM((levels + 1, 8, LANES), f32),
            pltpu.VMEM((5, 2, 8, LANES), f32),
            pltpu.VMEM((tx_num, 1, LANES), f32),
            pltpu.VMEM((tx_num, 1, LANES), f32),
            pltpu.VMEM((levels, 8, tx_num, LANES), f32),
            pltpu.VMEM((8, tx_num, LANES), f32),
            pltpu.VMEM((levels + 2, 8 + 2 * HALO, 8, LANES), f32),
            pltpu.VMEM((2, 3, 8 + 2 * HALO, 8, LANES), f32),
            pltpu.VMEM((tx_num, LANES), f32),
            pltpu.VMEM((2, batch * 8, LANES), f32),
            pltpu.VMEM((8, LANES), f32),
            dma((9,)),
            dma((CHUNKS,)), dma((CHUNKS,)),
            dma, dma,
            dma((8,)), dma((8,)),
            dma((8,)), dma((8,)),
            dma((CHUNKS, 8)), dma((CHUNKS, 8)),
            dma((8,)), dma((8,)),
            dma, dma,
        ],
        compiler_params=pltpu.CompilerParams(collective_id=0, has_side_effects=True),
    )(
        ensemble, diffusivity, vertical, weights,
        jnp.swapaxes(obs_value, 1, 2), jnp.swapaxes(obs_cell, 1, 2), obs_count,
    )
    increment, back = pl.pallas_call(
        functools.partial(hand_over, slots),
        out_shape=(
            jax.ShapeDtypeStruct(increment.shape, f32),
            jax.ShapeDtypeStruct((1, slots, tx_num), f32),
        ),
        in_specs=[vmem, vmem],
        out_specs=(vmem, vmem),
    )(increment, back)
    return increment, jnp.swapaxes(back, 1, 2)


def solution(mesh):
    placed = (
        P("tx", None, "ty", None),
        P("ty", "tx"),
        P(),
        P(),
        P(("ty", "tx"), None, None),
        P(("ty", "tx"), None, None),
        P(("ty", "tx"), None),
    )
    return jax.shard_map(
        functools.partial(shards, mesh.shape["ty"], mesh.shape["tx"]),
        mesh=mesh,
        in_specs=placed,
        out_specs=(P(None, "ty", "tx"), P(("ty", "tx"), None, None)),
        check_vma=False,
    )
```

```python
import functools

import jax
import jax.numpy as jnp
from jax import lax
from jax.experimental import pallas as pl
from jax.experimental.pallas import tpu as pltpu
from jax.sharding import PartitionSpec as P

STEPS = 4
HALO = 4
LANES = 128
GROUP = 16
CHUNKS = 4
MESH = pl.DeviceIdType.MESH
DIRS = ((-1, -1), (-1, 0), (-1, 1), (0, -1), (0, 1), (1, -1), (1, 0), (1, 1))
UP, DOWN = 1, 6
PLACE = (3, 2, 4, 0, 1, 3, 2, 4)


def split3(x):
    hi = x.astype(jnp.bfloat16)
    rest = x - hi.astype(jnp.float32)
    mid = rest.astype(jnp.bfloat16)
    low = (rest - mid.astype(jnp.float32)).astype(jnp.bfloat16)
    return hi, mid, low


def diffused(rows, coef, keep):
    width = len(rows)
    for step in range(1, STEPS + 1):
        fresh = [None] * width
        for i in range(step, width - step):
            beside = pltpu.roll(rows[i], 1, 2) + pltpu.roll(rows[i], LANES - 1, 2)
            fresh[i] = keep(i) * rows[i] + coef(i) * (beside + (rows[i - 1] + rows[i + 1]))
        rows = fresh
    return rows[STEPS : width - STEPS]


def kernel(
    ty_num, tx_num, ens, coef_in, vertical_in, weights_in, value_in, cell_in, count_in, inc_ref, back_ref,
    coef, vertical, weights, obs_value, obs_cell, obs_count, lines, pack,
    tiles, turned, edge_rows, strips, strips_in, field, strip_field, field_in, strip_field_in,
    got, out_rows, cur, cur_strip, spread_field, spread_strip, scale, stage, edge_sum, band,
    local_sem, ens_send, ens_recv, obs_send, obs_recv, fld_send, fld_recv,
    sfl_send, sfl_recv, row_send, row_recv, str_send, str_recv, ret_send, ret_recv,
):
    f32 = jnp.float32
    levels = tiles.shape[1]
    batch = min(16, tx_num)
    batches = tx_num // batch
    per = levels // CHUNKS
    part = tx_num // CHUNKS
    run = per * GROUP
    row, col = lax.axis_index("ty"), lax.axis_index("tx")

    def exists(move):
        down, right = move
        ok = None
        for shift, here, num in ((down, row, ty_num), (right, col, tx_num)):
            if shift:
                inside = here > 0 if shift < 0 else here < num - 1
                ok = inside if ok is None else jnp.logical_and(ok, inside)
        return ok

    def kept_rows(i):
        return {-1: pl.ds(HALO, HALO), 0: pl.ds(0, 8), 1: pl.ds(0, HALO)}[DIRS[i][0]]

    def peer(move):
        return (row + move[0], col + move[1])

    barrier = pltpu.get_barrier_semaphore()

    @pl.loop(1, tx_num)
    def _(i):
        pl.semaphore_signal(
            barrier, inc=1, device_id=(row, lax.rem(col + i, tx_num)), device_id_type=MESH
        )

    for move in DIRS:
        if move[0]:
            @pl.when(exists(move))
            def _():
                pl.semaphore_signal(barrier, inc=1, device_id=peer(move), device_id_type=MESH)

    mine = pltpu.make_async_copy(
        ens.at[0, :, :, pl.ds(pl.multiple_of(col * LANES, LANES), LANES)],
        tiles.at[col], local_sem.at[0],
    )
    small = [
        pltpu.make_async_copy(source, target, local_sem.at[3 + n])
        for n, (source, target) in enumerate((
            (value_in, obs_value), (cell_in, obs_cell), (count_in, obs_count),
            (coef_in, coef), (vertical_in, vertical), (weights_in, weights),
        ))
    ]
    for copy in small:
        copy.start()
    mine.start()

    awaited = tx_num - 1
    for move in DIRS:
        if move[0]:
            awaited = awaited + jnp.where(exists(move), 1, 0)
    pl.semaphore_wait(barrier, awaited)

    def obs_copy(to):
        return pltpu.make_async_remote_copy(
            src_ref=pack.at[to], dst_ref=got.at[col], send_sem=obs_send, recv_sem=obs_recv,
            device_id=(row, to), device_id_type=MESH,
        )

    def ens_copy(to, chunk):
        return pltpu.make_async_remote_copy(
            src_ref=ens.at[0, pl.ds(chunk * per, per), :, pl.ds(pl.multiple_of(to * LANES, LANES), LANES)],
            dst_ref=tiles.at[col, pl.ds(chunk * per, per)],
            send_sem=ens_send.at[chunk], recv_sem=ens_recv.at[chunk],
            device_id=(row, to), device_id_type=MESH,
        )

    def order(i):
        half = lax.div(i + 1, 2)
        return lax.rem(col + jnp.where(lax.rem(i, 2) == 1, half, tx_num - half), tx_num)

    def send_ens(chunk):
        @pl.loop(1, tx_num)
        def _(i):
            ens_copy(order(i), chunk).start()

    send_ens(0)

    for copy in small:
        copy.wait()
    live = lax.broadcasted_iota(jnp.int32, (8, tx_num), 0) < jnp.broadcast_to(obs_count[...], (8, tx_num))
    lines[...] = jnp.zeros(lines.shape, f32)
    lines[0:8, 0:tx_num] = obs_value[0]
    lines[8:16, 0:tx_num] = jnp.where(live, obs_cell[0], -1).astype(f32)
    pack[:, 0, :] = jnp.transpose(lines[...])[0:tx_num]
    mine_pack = pltpu.make_async_copy(pack.at[col], got.at[col], local_sem.at[1])
    mine_pack.start()

    @pl.loop(1, tx_num)
    def _(i):
        obs_copy(order(i)).start()

    for chunk in range(1, CHUNKS):
        send_ens(chunk)

    lane = lax.broadcasted_iota(jnp.int32, (8, LANES), 1)
    low_half = lax.rem(lane, GROUP) < GROUP // 2

    def into_strip(strip, tile, l, lane):
        moved = pltpu.roll(tile, (GROUP // 2 + GROUP * l) % LANES, tile.ndim - 1)
        return jnp.where(lax.div(lane, GROUP) == l, moved, strip)

    def strip_of(tile):
        out = jnp.where(lane < GROUP, pltpu.roll(tile, GROUP // 2, 1), 0.0)
        for width in (16, 32, 64):
            out = out + pltpu.roll(out, width, 1)
        return out

    field[levels] = coef[...]
    strip_field[1] = strip_of(coef[...])
    for k in range(tx_num):
        scale[k : k + 1, :] = jnp.full((1, LANES), weights[k], f32)

    for i, move in enumerate(DIRS):
        @pl.when(jnp.logical_not(exists(move)))
        def _():
            rows = kept_rows(i)
            size = HALO if move[0] else 8
            strip_field_in[PLACE[i], :, rows] = jnp.zeros((2, size, LANES), f32)
            strips_in[:, PLACE[i], rows] = jnp.zeros((CHUNKS, size, part, LANES), jnp.bfloat16)
            if i in (UP, DOWN):
                field_in[:, rows] = jnp.zeros((levels + 1, size, LANES), f32)
                edge_rows[:, rows] = jnp.zeros((levels, size, tx_num, LANES), jnp.bfloat16)

    mine_pack.wait()
    others = pl.ds(0, tx_num - 1)
    pltpu.make_async_remote_copy(
        src_ref=pack.at[others], dst_ref=got.at[others], send_sem=obs_send, recv_sem=obs_recv,
        device_id=(row, col), device_id_type=MESH,
    ).wait_recv()
    slots = got[:, 0, :]
    wide_lane = lax.broadcasted_iota(jnp.int32, (tx_num, LANES), 1)
    level_row, column, value = [], [], []
    for j in range(8):
        cell = jnp.broadcast_to(slots[:, 8 + j : 9 + j], (tx_num, LANES)).astype(jnp.int32)
        level_row.append(jnp.where((cell >> 7) == wide_lane, 1.0, 0.0).astype(f32))
        column.append((cell & 127) == wide_lane)
        value.append(jnp.where(column[-1], jnp.broadcast_to(slots[:, j : j + 1], (tx_num, LANES)), 0.0))
    pick = jnp.concatenate(level_row, axis=0)
    spread = jnp.concatenate(split3(jnp.concatenate(value, axis=0)), axis=1)
    summed = jnp.dot(
        jnp.transpose(pick).astype(jnp.bfloat16), spread, preferred_element_type=f32
    )
    forcing = summed[:, :LANES] + summed[:, LANES : 2 * LANES] + summed[:, 2 * LANES :]
    strip = jnp.zeros((8, LANES), f32)
    for l in range(levels):
        tile = forcing[8 * l : 8 * l + 8]
        field[l] = tile
        strip = into_strip(strip, tile, l, lane)
    strip_field[0] = strip

    def field_copy(i):
        rows = kept_rows(7 - i)
        return pltpu.make_async_remote_copy(
            src_ref=field.at[:, rows], dst_ref=field_in.at[:, rows],
            send_sem=fld_send.at[i], recv_sem=fld_recv.at[7 - i],
            device_id=peer(DIRS[i]), device_id_type=MESH,
        )

    def strip_field_copy(i):
        rows = kept_rows(7 - i)
        return pltpu.make_async_remote_copy(
            src_ref=strip_field.at[:, rows], dst_ref=strip_field_in.at[PLACE[7 - i], :, rows],
            send_sem=sfl_send.at[i], recv_sem=sfl_recv.at[7 - i],
            device_id=peer(DIRS[i]), device_id_type=MESH,
        )

    def rows_copy(i, chunk):
        cut = (pl.ds(chunk * per, per), kept_rows(7 - i))
        return pltpu.make_async_remote_copy(
            src_ref=turned.at[cut], dst_ref=edge_rows.at[cut],
            send_sem=row_send.at[chunk, i], recv_sem=row_recv.at[chunk, 7 - i],
            device_id=peer(DIRS[i]), device_id_type=MESH,
        )

    def strip_copy(i, chunk):
        rows = kept_rows(7 - i)
        return pltpu.make_async_remote_copy(
            src_ref=strips.at[chunk, rows], dst_ref=strips_in.at[chunk, PLACE[7 - i], rows],
            send_sem=str_send.at[chunk, i], recv_sem=str_recv.at[chunk, 7 - i],
            device_id=peer(DIRS[i]), device_id_type=MESH,
        )

    for i, move in enumerate(DIRS):
        @pl.when(exists(move))
        def _():
            strip_field_copy(i).start()
            if i in (UP, DOWN):
                field_copy(i).start()

    def arrived(copy_of, i):
        copy_of(7 - i).wait_recv()

    def edges(here, around, half):
        def joined(one, other):
            return jnp.where(half, one, other)

        return (
            (joined(here, around[1]), joined(around[2], around[4])),
            (joined(around[0], here), joined(around[3], around[2])),
        )

    def tall(i):
        return (0, i - HALO) if HALO <= i < HALO + 8 else (1, (i + HALO) % 8)

    def spread_rows(own, halo):
        pair = (own, halo)
        out = []
        for i in range(8 + 2 * HALO):
            which, r = tall(i)
            out.append(jnp.broadcast_to(pair[which][r : r + 1], (8, LANES)))
        return out

    def finish_fields():
        for i, move in enumerate(DIRS):
            @pl.when(exists(move))
            def _():
                arrived(strip_field_copy, i)
                if i in (UP, DOWN):
                    arrived(field_copy, i)
        for l in range(levels + 1):
            for i, line in enumerate(spread_rows(field[l], field_in[l])):
                spread_field[l, i] = line
                if l == levels:
                    spread_field[levels + 1, i] = 1.0 - 4.0 * line

        def repeated(strip, chunk):
            out = jnp.where(lane < run, pltpu.roll(strip, (-run * chunk) % LANES, 1), 0.0)
            width = run
            while width < LANES:
                out = out + pltpu.roll(out, width, 1)
                width *= 2
            return out

        for chunk in range(CHUNKS):
            both = edges(
                repeated(strip_field[0], chunk),
                [repeated(strip_field_in[i, 0], chunk) for i in range(5)], low_half,
            )
            for side in range(2):
                for i, line in enumerate(spread_rows(*both[side])):
                    spread_strip[side, 2 + chunk, i] = line
        both = edges(strip_field[1], [strip_field_in[i, 1] for i in range(5)], low_half)
        for side in range(2):
            for i, line in enumerate(spread_rows(*both[side])):
                spread_strip[side, 0, i] = line
                spread_strip[side, 1, i] = 1.0 - 4.0 * line

    def block(value):
        return value.astype(f32).reshape(value.shape[0] // 8, 8, LANES)

    def members(b):
        return pl.ds(pl.multiple_of(b * batch, batch), batch)

    def share(chunk):
        cut = pl.ds(chunk * per, per)
        pltpu.make_async_remote_copy(
            src_ref=tiles.at[others, cut], dst_ref=tiles.at[others, cut],
            send_sem=ens_send.at[chunk], recv_sem=ens_recv.at[chunk],
            device_id=(row, col), device_id_type=MESH,
        ).wait_recv()

        @pl.loop(0, batches)
        def _(b):
            for l in range(chunk * per, (chunk + 1) * per):
                slot = l % 2
                stage[slot] = tiles[members(b), l].astype(f32).reshape(batch * 8, LANES)
                for r in range(8):
                    turned[l, r, members(b)] = stage[slot, pl.ds(r, batch, stride=8)].astype(jnp.bfloat16)

        for i in (UP, DOWN):
            @pl.when(exists(DIRS[i]))
            def _():
                rows_copy(i, chunk).start()

    wide = lax.broadcasted_iota(jnp.int32, (part // 8, 8, LANES), 2)

    def share_strips(chunk):
        @pl.loop(0, 8)
        def _(r):
            out = jnp.zeros((part // 8, 8, LANES), f32)
            for n in range(CHUNKS):
                for l in range(per):
                    here = turned[chunk * per + l, r, pl.ds(n * part, part)]
                    out = into_strip(out, block(here), n * per + l, wide)
            strips[chunk, r] = out.reshape(part, LANES).astype(jnp.bfloat16)

        for i, move in enumerate(DIRS):
            @pl.when(exists(move))
            def _():
                strip_copy(i, chunk).start()

    def diffuse_main(chunk):
        for i in (UP, DOWN):
            @pl.when(exists(DIRS[i]))
            def _():
                arrived(functools.partial(rows_copy, chunk=chunk), i)

        @pl.loop(0, batches)
        def _(b):
            @pl.loop(chunk * per, (chunk + 1) * per)
            def _(l):
                rows = []
                for i in range(8 + 2 * HALO):
                    which, r = tall(i)
                    here = (turned, edge_rows)[which][l, r, members(b)]
                    rows.append(block(here) * spread_field[l, i])
                done = diffused(
                    rows, lambda i: spread_field[levels, i], lambda i: spread_field[levels + 1, i]
                )
                for r in range(8):
                    cur[l, r, members(b)] = done[r].reshape(batch, LANES)

    def diffuse_edges(chunk):
        for i, move in enumerate(DIRS):
            @pl.when(exists(move))
            def _():
                arrived(functools.partial(strip_copy, chunk=chunk), i)
        half = lax.rem(wide, GROUP) < GROUP // 2
        results = []
        for side in range(2):
            rows = []
            for i in range(8 + 2 * HALO):
                which, r = tall(i)
                here = block(strips[chunk, r])
                around = [block(strips_in[chunk, n, r]) for n in range(5)]
                rows.append(edges(here, around, half)[side][which] * spread_strip[side, 2 + chunk, i])
            results.append(
                diffused(rows, lambda i: spread_strip[side, 0, i], lambda i: spread_strip[side, 1, i])
            )
        for r in range(8):
            both = jnp.where(half, results[0][r], results[1][r])
            cur_strip[chunk, r] = both.reshape(part, LANES)

    mine.wait()
    share(0)
    share_strips(0)
    finish_fields()
    for chunk in range(1, CHUNKS):
        if chunk == CHUNKS - 1:
            for early in range(CHUNKS - 3):
                diffuse_main(early)
                diffuse_edges(early)
        share(chunk)
        share_strips(chunk)
    for chunk in range(CHUNKS - 3, CHUNKS):
        diffuse_main(chunk)
        diffuse_edges(chunk)

    bands = []
    strip_level = lax.rem(lax.div(lane, GROUP), per)
    for chunk in range(CHUNKS):
        for other in range(CHUNKS):
            for shift in range(1 - per, per):
                line = None
                for l in range(max(0, -shift), min(per, per - shift)):
                    target, source = chunk * per + l, other * per + l + shift
                    if abs(target - source) <= 2:
                        line = jnp.zeros((8, LANES), f32) if line is None else line
                        line = jnp.where(strip_level == l, vertical[target, source], line)
                if line is not None:
                    bands.append((chunk, other, shift))
                    band[len(bands) - 1] = line
    strip_scale = block(scale[pl.ds(0, part)])
    for n in range(1, CHUNKS):
        strip_scale = jnp.where(lax.div(wide, run) == n, block(scale[pl.ds(n * part, part)]), strip_scale)

    def mixed(parts, l):
        total = None
        for m in range(max(0, l - 2), min(levels, l + 3)):
            term = vertical[l, m] * parts[m]
            total = term if total is None else total + term
        return total

    def folded(total):
        return jnp.sum(jnp.sum(total, axis=0), axis=0, keepdims=True)

    @pl.loop(0, 8)
    def _(r):
        sums = [jnp.zeros((batch // 8, 8, LANES), f32)] * levels
        for b in range(batches):
            some = pl.ds(b * batch, batch)
            factor = block(scale[some])
            parts = [block(cur[m, r, some]) for m in range(levels)]
            for l in range(levels):
                sums[l] = sums[l] + (factor * block(turned[l, r, some])) * mixed(parts, l)
        for l in range(levels):
            inc_ref[l, pl.ds(r, 1)] = folded(sums[l])
        lines_of = [block(cur_strip[n, r]) for n in range(CHUNKS)]
        totals = [jnp.zeros((part // 8, 8, LANES), f32)] * CHUNKS
        for n, (chunk, other, shift) in enumerate(bands):
            moved = lines_of[other]
            if shift:
                moved = pltpu.roll(moved, (-GROUP * shift) % LANES, 2)
            totals[chunk] = totals[chunk] + band[n] * moved
        for chunk in range(CHUNKS):
            weighted = (strip_scale * block(strips[chunk, r])) * totals[chunk]
            edge_sum[chunk, pl.ds(r, 1)] = folded(weighted)

    edge_sums = []
    for chunk in range(CHUNKS):
        edge, width = edge_sum[chunk], LANES // 2
        while width >= run:
            edge = edge + pltpu.roll(edge, width, 1)
            width //= 2
        edge_sums.append(edge)

    increment = []
    for l in range(levels):
        edge = pltpu.roll(edge_sums[l // per], (LANES - GROUP // 2 - GROUP * (l % per)) % LANES, 1)
        increment.append(jnp.where((lane < HALO) | (lane >= LANES - HALO), edge, inc_ref[l]))
        inc_ref[l] = increment[-1]

    source = jnp.concatenate(increment + [jnp.zeros((LANES - 8 * levels, LANES), f32)], axis=0)
    taken = jnp.dot(
        pick.astype(jnp.bfloat16), jnp.concatenate(split3(source), axis=1),
        preferred_element_type=f32,
    )
    taken = taken[:, :LANES] + taken[:, LANES : 2 * LANES] + taken[:, 2 * LANES :]
    answer = jnp.zeros((tx_num, LANES), f32)
    for j in range(8):
        part = jnp.where(column[j], taken[tx_num * j : tx_num * (j + 1)], 0.0)
        answer = jnp.where(wide_lane == j, jnp.sum(part, axis=1, keepdims=True), answer)
    out_rows[:, 0, :] = answer

    def back_copy(to):
        return pltpu.make_async_remote_copy(
            src_ref=out_rows.at[to], dst_ref=back_ref.at[col],
            send_sem=ret_send, recv_sem=ret_recv, device_id=(row, to), device_id_type=MESH,
        )

    mine_back = pltpu.make_async_copy(out_rows.at[col], back_ref.at[col], local_sem.at[2])
    mine_back.start()

    @pl.loop(1, tx_num)
    def _(i):
        back_copy(order(i)).start()

    pltpu.make_async_remote_copy(
        src_ref=pack.at[others], dst_ref=got.at[others], send_sem=obs_send, recv_sem=obs_recv,
        device_id=(row, col), device_id_type=MESH,
    ).wait_send()
    for chunk in range(CHUNKS):
        cut = pl.ds(chunk * per, per)
        pltpu.make_async_remote_copy(
            src_ref=tiles.at[others, cut], dst_ref=tiles.at[others, cut],
            send_sem=ens_send.at[chunk], recv_sem=ens_recv.at[chunk],
            device_id=(row, col), device_id_type=MESH,
        ).wait_send()
    for i, move in enumerate(DIRS):
        @pl.when(exists(move))
        def _():
            strip_field_copy(i).wait_send()
            for chunk in range(CHUNKS):
                strip_copy(i, chunk).wait_send()
            if i in (UP, DOWN):
                field_copy(i).wait_send()
                for chunk in range(CHUNKS):
                    rows_copy(i, chunk).wait_send()
    mine_back.wait()
    pltpu.make_async_remote_copy(
        src_ref=out_rows.at[others], dst_ref=back_ref.at[others],
        send_sem=ret_send, recv_sem=ret_recv, device_id=(row, col), device_id_type=MESH,
    ).wait()


def hand_over(slots, inc_in, back_in, inc_out, back_out):
    inc_out[...] = inc_in[...]
    back_out[0] = jnp.transpose(back_in[:, 0, :])[:slots]


def shards(ty_num, tx_num, ensemble, diffusivity, vertical, weights, obs_value, obs_cell, obs_count):
    levels = ensemble.shape[1]
    slots = obs_value.shape[2]
    batch, part = min(16, tx_num), tx_num // CHUNKS
    f32, bf16, dma = jnp.float32, jnp.bfloat16, pltpu.SemaphoreType.DMA
    vmem = pl.BlockSpec(memory_space=pltpu.VMEM)
    hbm = pl.BlockSpec(memory_space=pltpu.HBM)
    increment, back = pl.pallas_call(
        functools.partial(kernel, ty_num, tx_num),
        out_shape=(
            jax.ShapeDtypeStruct((levels, 8, LANES), f32),
            jax.ShapeDtypeStruct((tx_num, 1, LANES), f32),
        ),
        in_specs=[hbm] * 7,
        out_specs=(vmem, vmem),
        scratch_shapes=[
            pltpu.VMEM(diffusivity.shape, f32),
            pltpu.SMEM(vertical.shape, f32),
            pltpu.SMEM(weights.shape, f32),
            pltpu.VMEM((1, slots, tx_num), f32),
            pltpu.VMEM((1, slots, tx_num), jnp.int32),
            pltpu.VMEM(obs_count.shape, jnp.int32),
            pltpu.VMEM((LANES, LANES), f32),
            pltpu.VMEM((tx_num, 1, LANES), f32),
            pltpu.VMEM((tx_num, levels, 8, LANES), bf16),
            pltpu.VMEM((levels, 8, tx_num, LANES), bf16),
            pltpu.VMEM((levels, 8, tx_num, LANES), bf16),
            pltpu.VMEM((CHUNKS, 8, part, LANES), bf16),
            pltpu.VMEM((CHUNKS, 5, 8, part, LANES), bf16),
            pltpu.VMEM((levels + 1, 8, LANES), f32),
            pltpu.VMEM((2, 8, LANES), f32),
            pltpu.VMEM((levels + 1, 8, LANES), f32),
            pltpu.VMEM((5, 2, 8, LANES), f32),
            pltpu.VMEM((tx_num, 1, LANES), f32),
            pltpu.VMEM((tx_num, 1, LANES), f32),
            pltpu.VMEM((levels, 8, tx_num, LANES), f32),
            pltpu.VMEM((CHUNKS, 8, part, LANES), f32),
            pltpu.VMEM((levels + 2, 8 + 2 * HALO, 8, LANES), f32),
            pltpu.VMEM((2, 2 + CHUNKS, 8 + 2 * HALO, 8, LANES), f32),
            pltpu.VMEM((tx_num, LANES), f32),
            pltpu.VMEM((2, batch * 8, LANES), f32),
            pltpu.VMEM((CHUNKS, 8, LANES), f32),
            pltpu.VMEM((64, 8, LANES), f32),
            dma((9,)),
            dma((CHUNKS,)), dma((CHUNKS,)),
            dma, dma,
            dma((8,)), dma((8,)),
            dma((8,)), dma((8,)),
            dma((CHUNKS, 8)), dma((CHUNKS, 8)),
            dma((CHUNKS, 8)), dma((CHUNKS, 8)),
            dma, dma,
        ],
        compiler_params=pltpu.CompilerParams(collective_id=0, has_side_effects=True),
    )(
        ensemble, diffusivity, vertical, weights,
        jnp.swapaxes(obs_value, 1, 2), jnp.swapaxes(obs_cell, 1, 2), obs_count,
    )
    increment, back = pl.pallas_call(
        functools.partial(hand_over, slots),
        out_shape=(
            jax.ShapeDtypeStruct(increment.shape, f32),
            jax.ShapeDtypeStruct((1, slots, tx_num), f32),
        ),
        in_specs=[vmem, vmem],
        out_specs=(vmem, vmem),
    )(increment, back)
    return increment, jnp.swapaxes(back, 1, 2)


def solution(mesh):
    placed = (
        P("tx", None, "ty", None),
        P("ty", "tx"),
        P(),
        P(),
        P(("ty", "tx"), None, None),
        P(("ty", "tx"), None, None),
        P(("ty", "tx"), None),
    )
    return jax.shard_map(
        functools.partial(shards, mesh.shape["ty"], mesh.shape["tx"]),
        mesh=mesh,
        in_specs=placed,
        out_specs=(P(None, "ty", "tx"), P(("ty", "tx"), None, None)),
        check_vma=False,
    )
```

```python
import functools

import jax
import jax.numpy as jnp
from jax import lax
from jax.experimental import pallas as pl
from jax.experimental.pallas import tpu as pltpu
from jax.sharding import PartitionSpec as P

STEPS = 4
HALO = 4
LANES = 128
GROUP = 16
CHUNKS = 4
MESH = pl.DeviceIdType.MESH
DIRS = ((-1, -1), (-1, 0), (-1, 1), (0, -1), (0, 1), (1, -1), (1, 0), (1, 1))
UP, DOWN = 1, 6
PLACE = (3, 2, 4, 0, 1, 3, 2, 4)


def split3(x):
    hi = x.astype(jnp.bfloat16)
    rest = x - hi.astype(jnp.float32)
    mid = rest.astype(jnp.bfloat16)
    low = (rest - mid.astype(jnp.float32)).astype(jnp.bfloat16)
    return hi, mid, low


def diffused(rows, coef, keep):
    width = len(rows)
    for step in range(1, STEPS + 1):
        fresh = [None] * width
        for i in range(step, width - step):
            beside = pltpu.roll(rows[i], 1, 2) + pltpu.roll(rows[i], LANES - 1, 2)
            fresh[i] = keep(i) * rows[i] + coef(i) * (beside + (rows[i - 1] + rows[i + 1]))
        rows = fresh
    return rows[STEPS : width - STEPS]


def kernel(
    ty_num, tx_num, ens, coef_in, vertical_in, weights_in, value_in, cell_in, count_in, inc_ref, back_ref,
    coef, vertical, weights, obs_value, obs_cell, obs_count, lines, pack,
    tiles, turned, edge_rows, strips, strips_in, field, strip_field, field_in, strip_field_in,
    got, out_rows, cur, cur_strip, spread_field, spread_strip, scale, stage, edge_sum, band,
    local_sem, ens_send, ens_recv, obs_send, obs_recv, fld_send, fld_recv,
    sfl_send, sfl_recv, row_send, row_recv, str_send, str_recv, ret_send, ret_recv,
):
    f32 = jnp.float32
    levels = tiles.shape[1]
    batch = min(16, tx_num)
    batches = tx_num // batch
    per = levels // CHUNKS
    part = tx_num // CHUNKS
    run = per * GROUP
    row, col = lax.axis_index("ty"), lax.axis_index("tx")

    def exists(move):
        down, right = move
        ok = None
        for shift, here, num in ((down, row, ty_num), (right, col, tx_num)):
            if shift:
                inside = here > 0 if shift < 0 else here < num - 1
                ok = inside if ok is None else jnp.logical_and(ok, inside)
        return ok

    def kept_rows(i):
        return {-1: pl.ds(HALO, HALO), 0: pl.ds(0, 8), 1: pl.ds(0, HALO)}[DIRS[i][0]]

    def peer(move):
        return (row + move[0], col + move[1])

    barrier = pltpu.get_barrier_semaphore()

    @pl.loop(1, tx_num)
    def _(i):
        pl.semaphore_signal(
            barrier, inc=1, device_id=(row, lax.rem(col + i, tx_num)), device_id_type=MESH
        )

    for move in DIRS:
        if move[0]:
            @pl.when(exists(move))
            def _():
                pl.semaphore_signal(barrier, inc=1, device_id=peer(move), device_id_type=MESH)

    mine = pltpu.make_async_copy(
        ens.at[0, :, :, pl.ds(pl.multiple_of(col * LANES, LANES), LANES)],
        tiles.at[col], local_sem.at[0],
    )
    small = [
        pltpu.make_async_copy(source, target, local_sem.at[3 + n])
        for n, (source, target) in enumerate((
            (value_in, obs_value), (cell_in, obs_cell), (count_in, obs_count),
            (coef_in, coef), (vertical_in, vertical), (weights_in, weights),
        ))
    ]
    for copy in small:
        copy.start()
    mine.start()

    awaited = tx_num - 1
    for move in DIRS:
        if move[0]:
            awaited = awaited + jnp.where(exists(move), 1, 0)
    pl.semaphore_wait(barrier, awaited)

    def obs_copy(to):
        return pltpu.make_async_remote_copy(
            src_ref=pack.at[to], dst_ref=got.at[col], send_sem=obs_send, recv_sem=obs_recv,
            device_id=(row, to), device_id_type=MESH,
        )

    def ens_copy(to, chunk):
        return pltpu.make_async_remote_copy(
            src_ref=ens.at[0, pl.ds(chunk * per, per), :, pl.ds(pl.multiple_of(to * LANES, LANES), LANES)],
            dst_ref=tiles.at[col, pl.ds(chunk * per, per)],
            send_sem=ens_send.at[chunk], recv_sem=ens_recv.at[chunk],
            device_id=(row, to), device_id_type=MESH,
        )

    def order(i):
        centre, away = tx_num // 4 + tx_num // 2 * lax.rem(i, 2), lax.div(i + 2, 4)
        side = jnp.where(lax.rem(lax.div(i, 2), 2) == 1, away, tx_num - away)
        return lax.rem(col + centre + side, tx_num)

    def send_ens(chunk):
        @pl.loop(0, tx_num - 1)
        def _(i):
            ens_copy(order(i), chunk).start()

    send_ens(0)

    for copy in small:
        copy.wait()
    live = lax.broadcasted_iota(jnp.int32, (8, tx_num), 0) < jnp.broadcast_to(obs_count[...], (8, tx_num))
    lines[...] = jnp.zeros(lines.shape, f32)
    lines[0:8, 0:tx_num] = obs_value[0]
    lines[8:16, 0:tx_num] = jnp.where(live, obs_cell[0], -1).astype(f32)
    pack[:, 0, :] = jnp.transpose(lines[...])[0:tx_num]
    mine_pack = pltpu.make_async_copy(pack.at[col], got.at[col], local_sem.at[1])
    mine_pack.start()

    @pl.loop(0, tx_num - 1)
    def _(i):
        obs_copy(order(i)).start()

    for chunk in range(1, CHUNKS):
        send_ens(chunk)

    lane = lax.broadcasted_iota(jnp.int32, (8, LANES), 1)
    low_half = lax.rem(lane, GROUP) < GROUP // 2

    def into_strip(strip, tile, l, lane):
        moved = pltpu.roll(tile, (GROUP // 2 + GROUP * l) % LANES, tile.ndim - 1)
        return jnp.where(lax.div(lane, GROUP) == l, moved, strip)

    def strip_of(tile):
        out = jnp.where(lane < GROUP, pltpu.roll(tile, GROUP // 2, 1), 0.0)
        for width in (16, 32, 64):
            out = out + pltpu.roll(out, width, 1)
        return out

    field[levels] = coef[...]
    strip_field[1] = strip_of(coef[...])
    for k in range(tx_num):
        scale[k : k + 1, :] = jnp.full((1, LANES), weights[k], f32)

    for i, move in enumerate(DIRS):
        @pl.when(jnp.logical_not(exists(move)))
        def _():
            rows = kept_rows(i)
            size = HALO if move[0] else 8
            strip_field_in[PLACE[i], :, rows] = jnp.zeros((2, size, LANES), f32)
            strips_in[:, PLACE[i], rows] = jnp.zeros((CHUNKS, size, part, LANES), jnp.bfloat16)
            if i in (UP, DOWN):
                field_in[:, rows] = jnp.zeros((levels + 1, size, LANES), f32)
                edge_rows[:, rows] = jnp.zeros((levels, size, tx_num, LANES), jnp.bfloat16)

    mine_pack.wait()
    others = pl.ds(0, tx_num - 1)
    pltpu.make_async_remote_copy(
        src_ref=pack.at[others], dst_ref=got.at[others], send_sem=obs_send, recv_sem=obs_recv,
        device_id=(row, col), device_id_type=MESH,
    ).wait_recv()
    slots = got[:, 0, :]
    wide_lane = lax.broadcasted_iota(jnp.int32, (tx_num, LANES), 1)
    level_row, column, value = [], [], []
    for j in range(8):
        cell = jnp.broadcast_to(slots[:, 8 + j : 9 + j], (tx_num, LANES)).astype(jnp.int32)
        level_row.append(jnp.where((cell >> 7) == wide_lane, 1.0, 0.0).astype(f32))
        column.append((cell & 127) == wide_lane)
        value.append(jnp.where(column[-1], jnp.broadcast_to(slots[:, j : j + 1], (tx_num, LANES)), 0.0))
    pick = jnp.concatenate(level_row, axis=0)
    spread = jnp.concatenate(split3(jnp.concatenate(value, axis=0)), axis=1)
    summed = jnp.dot(
        jnp.transpose(pick).astype(jnp.bfloat16), spread, preferred_element_type=f32
    )
    forcing = summed[:, :LANES] + summed[:, LANES : 2 * LANES] + summed[:, 2 * LANES :]
    strip = jnp.zeros((8, LANES), f32)
    for l in range(levels):
        tile = forcing[8 * l : 8 * l + 8]
        field[l] = tile
        strip = into_strip(strip, tile, l, lane)
    strip_field[0] = strip

    def field_copy(i):
        rows = kept_rows(7 - i)
        return pltpu.make_async_remote_copy(
            src_ref=field.at[:, rows], dst_ref=field_in.at[:, rows],
            send_sem=fld_send.at[i], recv_sem=fld_recv.at[7 - i],
            device_id=peer(DIRS[i]), device_id_type=MESH,
        )

    def strip_field_copy(i):
        rows = kept_rows(7 - i)
        return pltpu.make_async_remote_copy(
            src_ref=strip_field.at[:, rows], dst_ref=strip_field_in.at[PLACE[7 - i], :, rows],
            send_sem=sfl_send.at[i], recv_sem=sfl_recv.at[7 - i],
            device_id=peer(DIRS[i]), device_id_type=MESH,
        )

    def rows_copy(i, chunk):
        cut = (pl.ds(chunk * per, per), kept_rows(7 - i))
        return pltpu.make_async_remote_copy(
            src_ref=turned.at[cut], dst_ref=edge_rows.at[cut],
            send_sem=row_send.at[chunk, i], recv_sem=row_recv.at[chunk, 7 - i],
            device_id=peer(DIRS[i]), device_id_type=MESH,
        )

    def strip_copy(i, chunk):
        rows = kept_rows(7 - i)
        return pltpu.make_async_remote_copy(
            src_ref=strips.at[chunk, rows], dst_ref=strips_in.at[chunk, PLACE[7 - i], rows],
            send_sem=str_send.at[chunk, i], recv_sem=str_recv.at[chunk, 7 - i],
            device_id=peer(DIRS[i]), device_id_type=MESH,
        )

    for i, move in enumerate(DIRS):
        @pl.when(exists(move))
        def _():
            strip_field_copy(i).start()
            if i in (UP, DOWN):
                field_copy(i).start()

    def arrived(copy_of, i):
        copy_of(7 - i).wait_recv()

    def edges(here, around, half):
        def joined(one, other):
            return jnp.where(half, one, other)

        return (
            (joined(here, around[1]), joined(around[2], around[4])),
            (joined(around[0], here), joined(around[3], around[2])),
        )

    def tall(i):
        return (0, i - HALO) if HALO <= i < HALO + 8 else (1, (i + HALO) % 8)

    def spread_rows(own, halo):
        pair = (own, halo)
        out = []
        for i in range(8 + 2 * HALO):
            which, r = tall(i)
            out.append(jnp.broadcast_to(pair[which][r : r + 1], (8, LANES)))
        return out

    def finish_fields():
        for i, move in enumerate(DIRS):
            @pl.when(exists(move))
            def _():
                arrived(strip_field_copy, i)
                if i in (UP, DOWN):
                    arrived(field_copy, i)
        for l in range(levels + 1):
            for i, line in enumerate(spread_rows(field[l], field_in[l])):
                spread_field[l, i] = line
                if l == levels:
                    spread_field[levels + 1, i] = 1.0 - 4.0 * line

        def repeated(strip, chunk):
            out = jnp.where(lane < run, pltpu.roll(strip, (-run * chunk) % LANES, 1), 0.0)
            width = run
            while width < LANES:
                out = out + pltpu.roll(out, width, 1)
                width *= 2
            return out

        for chunk in range(CHUNKS):
            both = edges(
                repeated(strip_field[0], chunk),
                [repeated(strip_field_in[i, 0], chunk) for i in range(5)], low_half,
            )
            for side in range(2):
                for i, line in enumerate(spread_rows(*both[side])):
                    spread_strip[side, 2 + chunk, i] = line
        both = edges(strip_field[1], [strip_field_in[i, 1] for i in range(5)], low_half)
        for side in range(2):
            for i, line in enumerate(spread_rows(*both[side])):
                spread_strip[side, 0, i] = line
                spread_strip[side, 1, i] = 1.0 - 4.0 * line

    def block(value):
        return value.astype(f32).reshape(value.shape[0] // 8, 8, LANES)

    def members(b):
        return pl.ds(pl.multiple_of(b * batch, batch), batch)

    def share(chunk):
        cut = pl.ds(chunk * per, per)
        pltpu.make_async_remote_copy(
            src_ref=tiles.at[others, cut], dst_ref=tiles.at[others, cut],
            send_sem=ens_send.at[chunk], recv_sem=ens_recv.at[chunk],
            device_id=(row, col), device_id_type=MESH,
        ).wait_recv()

        @pl.loop(0, batches)
        def _(b):
            for l in range(chunk * per, (chunk + 1) * per):
                slot = l % 2
                stage[slot] = tiles[members(b), l].astype(f32).reshape(batch * 8, LANES)
                for r in range(8):
                    turned[l, r, members(b)] = stage[slot, pl.ds(r, batch, stride=8)].astype(jnp.bfloat16)

        for i in (UP, DOWN):
            @pl.when(exists(DIRS[i]))
            def _():
                rows_copy(i, chunk).start()

    wide = lax.broadcasted_iota(jnp.int32, (part // 8, 8, LANES), 2)

    def share_strips(chunk):
        @pl.loop(0, 8)
        def _(r):
            out = jnp.zeros((part // 8, 8, LANES), f32)
            for n in range(CHUNKS):
                for l in range(per):
                    here = turned[chunk * per + l, r, pl.ds(n * part, part)]
                    out = into_strip(out, block(here), n * per + l, wide)
            strips[chunk, r] = out.reshape(part, LANES).astype(jnp.bfloat16)

        for i, move in enumerate(DIRS):
            @pl.when(exists(move))
            def _():
                strip_copy(i, chunk).start()

    def diffuse_main(chunk):
        for i in (UP, DOWN):
            @pl.when(exists(DIRS[i]))
            def _():
                arrived(functools.partial(rows_copy, chunk=chunk), i)

        @pl.loop(0, batches)
        def _(b):
            for l in range(chunk * per, (chunk + 1) * per):
                rows = []
                for i in range(8 + 2 * HALO):
                    which, r = tall(i)
                    here = (turned, edge_rows)[which][l, r, members(b)]
                    rows.append(block(here) * spread_field[l, i])
                done = diffused(
                    rows, lambda i: spread_field[levels, i], lambda i: spread_field[levels + 1, i]
                )
                for r in range(8):
                    cur[l, r, members(b)] = done[r].reshape(batch, LANES)

    def diffuse_edges(chunk):
        for i, move in enumerate(DIRS):
            @pl.when(exists(move))
            def _():
                arrived(functools.partial(strip_copy, chunk=chunk), i)
        half = lax.rem(wide, GROUP) < GROUP // 2
        results = []
        for side in range(2):
            rows = []
            for i in range(8 + 2 * HALO):
                which, r = tall(i)
                here = block(strips[chunk, r])
                around = [block(strips_in[chunk, n, r]) for n in range(5)]
                rows.append(edges(here, around, half)[side][which] * spread_strip[side, 2 + chunk, i])
            results.append(
                diffused(rows, lambda i: spread_strip[side, 0, i], lambda i: spread_strip[side, 1, i])
            )
        for r in range(8):
            both = jnp.where(half, results[0][r], results[1][r])
            cur_strip[chunk, r] = both.reshape(part, LANES)

    mine.wait()
    share(0)
    share_strips(0)
    finish_fields()
    for chunk in range(1, CHUNKS):
        if chunk == CHUNKS - 1:
            for early in range(CHUNKS - 3):
                diffuse_main(early)
                diffuse_edges(early)
        share(chunk)
        share_strips(chunk)
    for chunk in range(CHUNKS - 3, CHUNKS):
        diffuse_main(chunk)
        diffuse_edges(chunk)

    bands = []
    strip_level = lax.rem(lax.div(lane, GROUP), per)
    for chunk in range(CHUNKS):
        for other in range(CHUNKS):
            for shift in range(1 - per, per):
                line = None
                for l in range(max(0, -shift), min(per, per - shift)):
                    target, source = chunk * per + l, other * per + l + shift
                    if abs(target - source) <= 2:
                        line = jnp.zeros((8, LANES), f32) if line is None else line
                        line = jnp.where(strip_level == l, vertical[target, source], line)
                if line is not None:
                    bands.append((chunk, other, shift))
                    band[len(bands) - 1] = line
    strip_scale = block(scale[pl.ds(0, part)])
    for n in range(1, CHUNKS):
        strip_scale = jnp.where(lax.div(wide, run) == n, block(scale[pl.ds(n * part, part)]), strip_scale)

    def mixed(parts, l):
        total = None
        for m in range(max(0, l - 2), min(levels, l + 3)):
            term = vertical[l, m] * parts[m]
            total = term if total is None else total + term
        return total

    def folded(total):
        return jnp.sum(jnp.sum(total, axis=0), axis=0, keepdims=True)

    @pl.loop(0, 8)
    def _(r):
        sums = [jnp.zeros((batch // 8, 8, LANES), f32)] * levels
        for b in range(batches):
            some = pl.ds(b * batch, batch)
            factor = block(scale[some])
            parts = [block(cur[m, r, some]) for m in range(levels)]
            for l in range(levels):
                sums[l] = sums[l] + (factor * block(turned[l, r, some])) * mixed(parts, l)
        for l in range(levels):
            inc_ref[l, pl.ds(r, 1)] = folded(sums[l])
        lines_of = [block(cur_strip[n, r]) for n in range(CHUNKS)]
        totals = [jnp.zeros((part // 8, 8, LANES), f32)] * CHUNKS
        for n, (chunk, other, shift) in enumerate(bands):
            moved = lines_of[other]
            if shift:
                moved = pltpu.roll(moved, (-GROUP * shift) % LANES, 2)
            totals[chunk] = totals[chunk] + band[n] * moved
        for chunk in range(CHUNKS):
            weighted = (strip_scale * block(strips[chunk, r])) * totals[chunk]
            edge_sum[chunk, pl.ds(r, 1)] = folded(weighted)

    edge_sums = []
    for chunk in range(CHUNKS):
        edge, width = edge_sum[chunk], LANES // 2
        while width >= run:
            edge = edge + pltpu.roll(edge, width, 1)
            width //= 2
        edge_sums.append(edge)

    increment = []
    for l in range(levels):
        edge = pltpu.roll(edge_sums[l // per], (LANES - GROUP // 2 - GROUP * (l % per)) % LANES, 1)
        increment.append(jnp.where((lane < HALO) | (lane >= LANES - HALO), edge, inc_ref[l]))
        inc_ref[l] = increment[-1]

    source = jnp.concatenate(increment + [jnp.zeros((LANES - 8 * levels, LANES), f32)], axis=0)
    taken = jnp.dot(
        pick.astype(jnp.bfloat16), jnp.concatenate(split3(source), axis=1),
        preferred_element_type=f32,
    )
    taken = taken[:, :LANES] + taken[:, LANES : 2 * LANES] + taken[:, 2 * LANES :]
    answer = jnp.zeros((tx_num, LANES), f32)
    for j in range(8):
        part = jnp.where(column[j], taken[tx_num * j : tx_num * (j + 1)], 0.0)
        answer = jnp.where(wide_lane == j, jnp.sum(part, axis=1, keepdims=True), answer)
    out_rows[:, 0, :] = answer

    def back_copy(to):
        return pltpu.make_async_remote_copy(
            src_ref=out_rows.at[to], dst_ref=back_ref.at[col],
            send_sem=ret_send, recv_sem=ret_recv, device_id=(row, to), device_id_type=MESH,
        )

    mine_back = pltpu.make_async_copy(out_rows.at[col], back_ref.at[col], local_sem.at[2])
    mine_back.start()

    @pl.loop(0, tx_num - 1)
    def _(i):
        back_copy(order(i)).start()

    pltpu.make_async_remote_copy(
        src_ref=pack.at[others], dst_ref=got.at[others], send_sem=obs_send, recv_sem=obs_recv,
        device_id=(row, col), device_id_type=MESH,
    ).wait_send()
    for chunk in range(CHUNKS):
        cut = pl.ds(chunk * per, per)
        pltpu.make_async_remote_copy(
            src_ref=tiles.at[others, cut], dst_ref=tiles.at[others, cut],
            send_sem=ens_send.at[chunk], recv_sem=ens_recv.at[chunk],
            device_id=(row, col), device_id_type=MESH,
        ).wait_send()
    for i, move in enumerate(DIRS):
        @pl.when(exists(move))
        def _():
            strip_field_copy(i).wait_send()
            for chunk in range(CHUNKS):
                strip_copy(i, chunk).wait_send()
            if i in (UP, DOWN):
                field_copy(i).wait_send()
                for chunk in range(CHUNKS):
                    rows_copy(i, chunk).wait_send()
    mine_back.wait()
    pltpu.make_async_remote_copy(
        src_ref=out_rows.at[others], dst_ref=back_ref.at[others],
        send_sem=ret_send, recv_sem=ret_recv, device_id=(row, col), device_id_type=MESH,
    ).wait()


def hand_over(slots, inc_in, back_in, inc_out, back_out):
    inc_out[...] = inc_in[...]
    back_out[0] = jnp.transpose(back_in[:, 0, :])[:slots]


def shards(ty_num, tx_num, ensemble, diffusivity, vertical, weights, obs_value, obs_cell, obs_count):
    levels = ensemble.shape[1]
    slots = obs_value.shape[2]
    batch, part = min(16, tx_num), tx_num // CHUNKS
    f32, bf16, dma = jnp.float32, jnp.bfloat16, pltpu.SemaphoreType.DMA
    vmem = pl.BlockSpec(memory_space=pltpu.VMEM)
    hbm = pl.BlockSpec(memory_space=pltpu.HBM)
    increment, back = pl.pallas_call(
        functools.partial(kernel, ty_num, tx_num),
        out_shape=(
            jax.ShapeDtypeStruct((levels, 8, LANES), f32),
            jax.ShapeDtypeStruct((tx_num, 1, LANES), f32),
        ),
        in_specs=[hbm] * 7,
        out_specs=(vmem, vmem),
        scratch_shapes=[
            pltpu.VMEM(diffusivity.shape, f32),
            pltpu.SMEM(vertical.shape, f32),
            pltpu.SMEM(weights.shape, f32),
            pltpu.VMEM((1, slots, tx_num), f32),
            pltpu.VMEM((1, slots, tx_num), jnp.int32),
            pltpu.VMEM(obs_count.shape, jnp.int32),
            pltpu.VMEM((LANES, LANES), f32),
            pltpu.VMEM((tx_num, 1, LANES), f32),
            pltpu.VMEM((tx_num, levels, 8, LANES), bf16),
            pltpu.VMEM((levels, 8, tx_num, LANES), bf16),
            pltpu.VMEM((levels, 8, tx_num, LANES), bf16),
            pltpu.VMEM((CHUNKS, 8, part, LANES), bf16),
            pltpu.VMEM((CHUNKS, 5, 8, part, LANES), bf16),
            pltpu.VMEM((levels + 1, 8, LANES), f32),
            pltpu.VMEM((2, 8, LANES), f32),
            pltpu.VMEM((levels + 1, 8, LANES), f32),
            pltpu.VMEM((5, 2, 8, LANES), f32),
            pltpu.VMEM((tx_num, 1, LANES), f32),
            pltpu.VMEM((tx_num, 1, LANES), f32),
            pltpu.VMEM((levels, 8, tx_num, LANES), f32),
            pltpu.VMEM((CHUNKS, 8, part, LANES), f32),
            pltpu.VMEM((levels + 2, 8 + 2 * HALO, 8, LANES), f32),
            pltpu.VMEM((2, 2 + CHUNKS, 8 + 2 * HALO, 8, LANES), f32),
            pltpu.VMEM((tx_num, LANES), f32),
            pltpu.VMEM((2, batch * 8, LANES), f32),
            pltpu.VMEM((CHUNKS, 8, LANES), f32),
            pltpu.VMEM((64, 8, LANES), f32),
            dma((9,)),
            dma((CHUNKS,)), dma((CHUNKS,)),
            dma, dma,
            dma((8,)), dma((8,)),
            dma((8,)), dma((8,)),
            dma((CHUNKS, 8)), dma((CHUNKS, 8)),
            dma((CHUNKS, 8)), dma((CHUNKS, 8)),
            dma, dma,
        ],
        compiler_params=pltpu.CompilerParams(collective_id=0, has_side_effects=True),
    )(
        ensemble, diffusivity, vertical, weights,
        jnp.swapaxes(obs_value, 1, 2), jnp.swapaxes(obs_cell, 1, 2), obs_count,
    )
    increment, back = pl.pallas_call(
        functools.partial(hand_over, slots),
        out_shape=(
            jax.ShapeDtypeStruct(increment.shape, f32),
            jax.ShapeDtypeStruct((1, slots, tx_num), f32),
        ),
        in_specs=[vmem, vmem],
        out_specs=(vmem, vmem),
    )(increment, back)
    return increment, jnp.swapaxes(back, 1, 2)


def solution(mesh):
    placed = (
        P("tx", None, "ty", None),
        P("ty", "tx"),
        P(),
        P(),
        P(("ty", "tx"), None, None),
        P(("ty", "tx"), None, None),
        P(("ty", "tx"), None),
    )
    return jax.shard_map(
        functools.partial(shards, mesh.shape["ty"], mesh.shape["tx"]),
        mesh=mesh,
        in_specs=placed,
        out_specs=(P(None, "ty", "tx"), P(("ty", "tx"), None, None)),
        check_vma=False,
    )
```
